512 devices in a mesh: lat: 32 (over x, z), lev: 16 (over y, core).
Axes of the slice: x: 4, y: 8, z: 8, core: 2. Of those that a mesh axis runs over, the one named last changes fastest.
Arguments:
- fields: float32 [2, 128, 64, 3072], P(None, 'lat', 'lev'), may hold values from -6 to 6
- courant: bfloat16 [2, 128, 64, 3072], P(None, 'lat', 'lev'), may hold values from -0.3984375 to 0.3984375
- cutoffs: int32 [128], replicated, may hold values from 1 to 1536, as said below
- surface: float32 [128, 3072], P('lat'), may hold values from -6 to 6
- remap_weights: float32 [64, 64], replicated, may hold values from -0.25 to 0.75
Outputs:
- remapped: float32 [2, 128, 64, 3072], P(None, 'lat', None, 'lev')
- geopotential: float32 [128, 64, 3072], P('lat', None, 'lev')
The draws below stay inside these ranges and needn't reach their ends.
Inputs may be any that keep to these rules, and one draw needn't show every extreme that they name: cutoffs[j] is 1536 except on the first and the last 16 latitudes, where it lies between 1 and 127; it equals 127 on some latitude among the first 16.
All inputs are finite; a program needn't handle non-finite values.
Results may differ from the reference program's by a relative error of at most 0.0003.
Values may be sent and summed in bfloat16 or wider, within the bound.
A program may use at most 64 MiB of HBM per device.

```python
import math
import jax
import jax.numpy as jnp
from jax import lax

NLON = 3072
NLEV = 64
KMAX = 128
NLAT = 128
POLAR_ROWS = 16


def draw_cutoffs(key, part):
    latitude = jnp.arange(NLAT, dtype=jnp.int32)
    polar_band = (latitude < POLAR_ROWS) | (latitude >= NLAT - POLAR_ROWS)
    random_cut = jax.random.randint(jax.random.fold_in(key, 11), (NLAT,), 1, KMAX, dtype=jnp.int32)
    position = jax.random.randint(jax.random.fold_in(key, 12), (), 0, POLAR_ROWS, dtype=jnp.int32)
    random_cut = jnp.where(latitude == position, KMAX - 1, random_cut)
    return jnp.where(polar_band, random_cut, NLON // 2).astype(jnp.int32)


def draw_remap_weights(key, part):
    noise_draw = jax.random.truncated_normal(jax.random.fold_in(key, 22), -4.0, 4.0, (NLEV, NLEV), jnp.float32)
    return (0.5 * jnp.eye(NLEV, dtype=jnp.float32) + noise_draw * (0.5 / math.sqrt(NLEV))).astype(jnp.float32)


def block_scale(stream_key, extent, split, low, largest):
    def one(dim, blocks):
        draws = jax.random.uniform(jax.random.fold_in(jax.random.fold_in(stream_key, 6), dim), (blocks,), jnp.float32, low / len(split), largest / len(split))
        return jnp.repeat(jnp.exp(draws), extent[dim] // blocks).reshape((-1,) + (1,) * (len(extent) - dim - 1))

    loudness = one(*split[0])
    for cut in split[1:]:
        loudness = loudness * one(*cut)
    return loudness


def bell_draw(key, dims, deviation, limit, cuts=(), kind=jnp.bfloat16):
    drawn = jax.random.normal(key, dims, jnp.float32) * deviation
    if len(cuts) > 0:
        drawn = block_scale(key, dims, cuts, -0.22, 0.18) * drawn
    return jnp.clip(drawn, min=-limit, max=limit).astype(kind)


def setup_inputs(seed: int = 0) -> dict:
    splits = jax.random.split(jax.random.key(seed), 6)
    return {
        "fields": bell_draw(splits[0], (2, NLAT, NLEV, NLON), 1.0, 6.0, ((1, 32), (2, 16)), jnp.float32),
        "courant": jnp.clip(jax.random.uniform(splits[1], (2, NLAT, NLEV, NLON), jnp.float32, -0.3984375, 0.3984375) * block_scale(splits[1], (2, NLAT, NLEV, NLON), ((1, 32), (2, 16)), -0.4, 0.0), -0.3984375, 0.3984375).astype(jnp.bfloat16),
        "cutoffs": draw_cutoffs(jax.random.fold_in(splits[5], 71), 0),
        "surface": bell_draw(splits[3], (NLAT, NLON), 1.0, 6.0, ((0, 32),), jnp.float32),
        "remap_weights": draw_remap_weights(jax.random.fold_in(splits[5], 71), 0),
    }


def lon_part(values, east_wind):
    interface = (7.0 * (values + jnp.roll(values, -1, -1)) - (jnp.roll(values, 1, -1) + jnp.roll(values, -2, -1))) / 12.0
    face_wind = 0.5 * (east_wind + jnp.roll(east_wind, -1, -1))
    flux_faces = face_wind * interface
    return flux_faces - jnp.roll(flux_faces, 1, -1)


def lat_part(padded, north_wind):
    row_count = padded.shape[1] - 4
    interface = (7.0 * (padded[:, 1:row_count + 2] + padded[:, 2:row_count + 3]) - (padded[:, 0:row_count + 1] + padded[:, 3:row_count + 4])) / 12.0
    face_wind = 0.5 * (north_wind[0:row_count + 1] + north_wind[1:row_count + 2])
    flux_faces = face_wind * interface
    return flux_faces[:, 1:] - flux_faces[:, :-1]


def polar_filter(values, cutoffs):
    spectrum = jnp.fft.rfft(values, axis=-1)
    wave_numbers = jnp.arange(NLON // 2 + 1)
    kept_modes = wave_numbers[None, :] <= cutoffs[:, None]
    lowpass = jnp.fft.irfft(spectrum * kept_modes[None], n=NLON, axis=-1).astype(values.dtype)
    return jnp.where((cutoffs < NLON // 2)[None, :, None], lowpass, values)


def reference(fields, courant, cutoffs, surface, remap_weights):
    def per_level(level_index):
        values = lax.dynamic_index_in_dim(fields, level_index, 2, keepdims=False)
        winds = lax.dynamic_index_in_dim(courant, level_index, 2, keepdims=False).astype(jnp.float32)
        east_wind = winds[0]
        north_wind = jnp.pad(winds[1], ((1, 1), (0, 0)))
        for repeat in range(2):
            padded = jnp.pad(values, ((0, 0), (2, 2), (0, 0)))
            values = values - lon_part(values, east_wind) - lat_part(padded, north_wind)
            values = polar_filter(values, cutoffs)
        return values

    transported = lax.map(per_level, jnp.arange(NLEV, dtype=jnp.int32))
    remapped = jnp.einsum('pk,kfjn->fjpn', remap_weights, transported, precision=lax.Precision.HIGHEST)
    heat_rows = transported[:, 1]
    upward = jnp.cumsum(heat_rows[::-1], axis=0)[::-1]
    geo_scale = NLEV ** -0.5
    geo_levels = surface[None] + geo_scale * (upward - 0.5 * heat_rows)
    geopotential = jnp.transpose(geo_levels, (1, 0, 2))
    return remapped, geopotential
```

```python
import functools

import jax
import jax.numpy as jnp
import numpy as np
from jax import lax
from jax.experimental import pallas as pl
from jax.experimental.pallas import tpu as pltpu
from jax.sharding import PartitionSpec as P

MESH = pl.DeviceIdType.MESH
KMAX = 128
SEG = 256
F32 = jnp.float32
BF16 = jnp.bfloat16


def split_bf16(table):
    high = table.astype(np.float32).astype(jnp.bfloat16)
    low = (table - high.astype(np.float64)).astype(np.float32).astype(jnp.bfloat16)
    return np.stack([high, low])


def fourier_tables(length):
    waves = np.arange(KMAX)
    phase = (np.arange(SEG)[:, None] * waves[None, :]) % length
    angle = phase * (2.0 * np.pi / length)
    inner = np.concatenate([np.cos(angle), np.sin(angle)], axis=1)
    segments = length // SEG
    outer = (np.arange(segments)[:, None] * waves[None, :]) % segments
    outer = outer * (2.0 * np.pi / segments)
    turn = np.stack([np.cos(outer), np.sin(outer)], axis=1).astype(np.float32)
    return split_bf16(inner), split_bf16(inner.T), turn.reshape(2 * segments, KMAX)


def halves(x):
    high = x.astype(BF16)
    return high, (x - high.astype(F32)).astype(BF16)


def dot3(x, high, low):
    x_high, x_low = halves(x)
    out = jnp.dot(x_high, high, preferred_element_type=F32)
    out += jnp.dot(x_low, high, preferred_element_type=F32)
    return out + jnp.dot(x_high, low, preferred_element_type=F32)


def zonal(u, coef):
    length = u.shape[-1]
    pair = u + pltpu.roll(u, length - 1, 1)
    face = 8.0 * pair - (pltpu.roll(pair, 1, 1) + pltpu.roll(pair, length - 1, 1))
    flux = coef * face
    return u - (flux - pltpu.roll(flux, 1, 1))


def kernel(
    n_lat, n_lev, polar,
    fields, courant, cutoffs, surface, weights, fwd, inv, turn,
    out, geo,
    cv, cut, surf, wv, fwd_v, inv_v, turn_v,
    u, z, coef_x, coef_y, halo, cy_halo, send, recv,
    in_sem, halo_send, halo_recv, cy_send, cy_recv, a2a_send, a2a_recv,
):
    ilat, ilev = lax.axis_index("lat"), lax.axis_index("lev")
    rows, length = u.shape[0], u.shape[2]
    levs = u.shape[1] // 2
    segments = length // SEG
    pair_id, parity = lax.div(ilev, 2), lax.rem(ilev, 2)
    width = 3 * 128

    loads = [
        pltpu.make_async_copy(fields.at[0], u.at[:, 0:levs, :], in_sem.at[0]),
        pltpu.make_async_copy(fields.at[1], u.at[:, levs : 2 * levs, :], in_sem.at[1]),
        pltpu.make_async_copy(courant, cv, in_sem.at[2]),
        pltpu.make_async_copy(cutoffs, cut, in_sem.at[3]),
        pltpu.make_async_copy(
            surface.at[:, pl.ds(pl.multiple_of(pair_id * width, 128), width)], surf, in_sem.at[4]
        ),
        pltpu.make_async_copy(weights, wv, in_sem.at[5]),
        pltpu.make_async_copy(fwd, fwd_v, in_sem.at[6]),
        pltpu.make_async_copy(inv, inv_v, in_sem.at[7]),
        pltpu.make_async_copy(turn, turn_v, in_sem.at[8]),
    ]
    for load in loads:
        load.start()

    has_minus, has_plus = ilat > 0, ilat < n_lat - 1
    barrier = pltpu.get_barrier_semaphore()

    @pl.when(has_minus)
    def _():
        pl.semaphore_signal(barrier, inc=1, device_id={"lat": ilat - 1}, device_id_type=MESH)

    @pl.when(has_plus)
    def _():
        pl.semaphore_signal(barrier, inc=1, device_id={"lat": ilat + 1}, device_id_type=MESH)

    @pl.loop(1, n_lev)
    def _(step):
        pl.semaphore_signal(
            barrier, inc=1, device_id={"lev": lax.rem(ilev + step, n_lev)}, device_id_type=MESH
        )

    for load in loads:
        load.wait()

    neighbours = has_minus.astype(jnp.int32) + has_plus.astype(jnp.int32)
    pl.semaphore_wait(barrier, n_lev - 1 + neighbours)

    def to_plus(phase):
        return pltpu.make_async_remote_copy(
            src_ref=u.at[rows - 2 : rows], dst_ref=halo.at[phase, 0],
            send_sem=halo_send.at[phase, 0], recv_sem=halo_recv.at[phase, 0],
            device_id={"lat": ilat + 1}, device_id_type=MESH,
        )

    def to_minus(phase):
        return pltpu.make_async_remote_copy(
            src_ref=u.at[0:2], dst_ref=halo.at[phase, 1],
            send_sem=halo_send.at[phase, 1], recv_sem=halo_recv.at[phase, 1],
            device_id={"lat": ilat - 1}, device_id_type=MESH,
        )

    def cy_plus():
        return pltpu.make_async_remote_copy(
            src_ref=cv.at[1, rows - 1], dst_ref=cy_halo.at[0],
            send_sem=cy_send.at[0], recv_sem=cy_recv.at[0],
            device_id={"lat": ilat + 1}, device_id_type=MESH,
        )

    def cy_minus():
        return pltpu.make_async_remote_copy(
            src_ref=cv.at[1, 0], dst_ref=cy_halo.at[1],
            send_sem=cy_send.at[1], recv_sem=cy_recv.at[1],
            device_id={"lat": ilat - 1}, device_id_type=MESH,
        )

    def both(x):
        return jnp.concatenate([x, x], axis=0)

    def exchange_start(phase):
        @pl.when(has_plus)
        def _():
            to_plus(phase).start()
            if phase == 0:
                cy_plus().start()

        @pl.when(has_minus)
        def _():
            to_minus(phase).start()
            if phase == 0:
                cy_minus().start()

        @pl.when(jnp.logical_not(has_minus))
        def _():
            halo[phase, 0] = jnp.zeros(halo.shape[2:], F32)
            if phase == 0:
                cy_halo[0] = jnp.zeros(cy_halo.shape[1:], BF16)

        @pl.when(jnp.logical_not(has_plus))
        def _():
            halo[phase, 1] = jnp.zeros(halo.shape[2:], F32)
            if phase == 0:
                cy_halo[1] = jnp.zeros(cy_halo.shape[1:], BF16)

    def exchange_wait(phase):
        @pl.when(has_minus)
        def _():
            to_plus(phase).wait_recv()
            to_minus(phase).wait_send()
            if phase == 0:
                cy_plus().wait_recv()
                cy_minus().wait_send()

        @pl.when(has_plus)
        def _():
            to_minus(phase).wait_recv()
            to_plus(phase).wait_send()
            if phase == 0:
                cy_minus().wait_recv()
                cy_plus().wait_send()

    def cy_row(j):
        if j < 0:
            return both(cy_halo[0].astype(F32))
        if j >= rows:
            return both(cy_halo[1].astype(F32))
        return both(cv[1, j].astype(F32))

    def meridional(phase):
        piece = 512

        @pl.loop(0, length // piece)
        def _(c):
            at = pl.ds(pl.multiple_of(c * piece, 128), piece)
            full = [halo[phase, 0, 0, :, at], halo[phase, 0, 1, :, at]]
            full += [u[j, :, at] for j in range(rows)]
            full += [halo[phase, 1, 0, :, at], halo[phase, 1, 1, :, at]]
            before = None
            for face in range(rows + 1):
                a, b, d, e = full[face : face + 4]
                flux = coef_y[face, :, at] * (7.0 * (b + d) - (a + e))
                if before is not None:
                    u[face - 1, :, at] = z[face - 1, :, at] - (flux - before)
                before = flux

    def low_pass():
        x = jnp.concatenate([u[j] for j in range(rows)], axis=0)
        count = x.shape[0]
        stacked = jnp.concatenate([x[:, q * SEG : (q + 1) * SEG] for q in range(segments)], axis=0)
        part = dot3(stacked, fwd_v[0], fwd_v[1])
        real = jnp.zeros((count, KMAX), F32)
        imag = jnp.zeros((count, KMAX), F32)
        for q in range(segments):
            p = part[q * count : (q + 1) * count, 0:KMAX]
            s = part[q * count : (q + 1) * count, KMAX : 2 * KMAX]
            c_q, s_q = turn_v[2 * q : 2 * q + 1, :], turn_v[2 * q + 1 : 2 * q + 2, :]
            real += c_q * p - s_q * s
            imag += s_q * p + c_q * s
        wave = lax.broadcasted_iota(jnp.int32, (2 * levs, KMAX), 1)
        double = jnp.where(wave == 0, 1.0 / length, 2.0 / length).astype(F32)
        weight = jnp.concatenate(
            [jnp.where(wave <= cut[ilat * rows + j], double, 0.0) for j in range(rows)], axis=0
        )
        real, imag = real * weight, imag * weight
        spread = []
        for q in range(segments):
            c_q, s_q = turn_v[2 * q : 2 * q + 1, :], turn_v[2 * q + 1 : 2 * q + 2, :]
            spread.append(
                jnp.concatenate([real * c_q + imag * s_q, imag * c_q - real * s_q], axis=1)
            )
        back = dot3(jnp.concatenate(spread, axis=0), inv_v[0], inv_v[1])
        for q in range(segments):
            for j in range(rows):
                at = q * count + j * 2 * levs
                u[j, :, q * SEG : (q + 1) * SEG] = back[at : at + 2 * levs]

    exchange_start(0)
    for j in range(rows):
        cx = both(cv[0, j].astype(F32))
        coef_x[j] = (cx + pltpu.roll(cx, length - 1, 1)) * (1.0 / 24.0)
    for j in range(rows):
        z[j] = zonal(u[j], coef_x[j])
    for face in range(1, rows):
        coef_y[face] = (cy_row(face - 1) + cy_row(face)) * (1.0 / 24.0)
    exchange_wait(0)
    for face in (0, rows):
        coef_y[face] = (cy_row(face - 1) + cy_row(face)) * (1.0 / 24.0)
    is_polar = jnp.logical_or(ilat < polar, ilat >= n_lat - polar)
    meridional(0)
    pl.when(is_polar)(low_pass)
    exchange_start(1)
    for j in range(rows):
        z[j] = zonal(u[j], coef_x[j])
    exchange_wait(1)
    meridional(1)
    pl.when(is_polar)(low_pass)

    lane = lax.broadcasted_iota(jnp.int32, (2 * levs, 128), 1)
    low_lane = lane < 64

    @pl.loop(0, n_lev // 2)
    def _(e):
        def tile(j, t):
            return u[j, :, pl.ds(pl.multiple_of(e * width + t * 128, 128), 128)]

        for j in range(rows):
            send[2 * e, j] = tile(j, 0)
            send[2 * e + 1, j] = tile(j, 2)
        for j in range(0, rows, 2):
            one, two = tile(j, 1), tile(j + 1, 1)
            send[2 * e, rows + j // 2] = jnp.where(low_lane, one, pltpu.roll(two, 64, 1))
            send[2 * e + 1, rows + j // 2] = jnp.where(low_lane, pltpu.roll(one, 64, 1), two)

    def offset(step):
        half = lax.div(step + 1, 2)
        return n_lev // 2 + jnp.where(lax.rem(step, 2) == 1, -half, half)

    def column_copy(step):
        other = lax.rem(ilev + offset(step), n_lev)
        return pltpu.make_async_remote_copy(
            src_ref=send.at[other], dst_ref=recv.at[ilev],
            send_sem=a2a_send.at[step], recv_sem=a2a_recv.at[step],
            device_id={"lev": other}, device_id_type=MESH,
        )

    @pl.loop(0, n_lev - 1)
    def _(step):
        column_copy(step).start()

    recv[ilev] = send[ilev]

    count = n_lev * levs
    depth = n_lev * 2 * levs
    source = lax.broadcasted_iota(jnp.int32, (count, depth), 1)
    target = lax.broadcasted_iota(jnp.int32, (count, depth), 0)
    level = lax.div(source, 2 * levs) * levs + lax.rem(source, levs)
    is_heat = lax.rem(source, 2 * levs) >= levs
    pick = (level == target).astype(F32)
    scale = count**-0.5
    deeper = jnp.where(level > target, scale, jnp.where(level == target, 0.5 * scale, 0.0))
    w = wv[...]
    w_high = w.astype(BF16)
    rest = w - w_high.astype(F32)
    w_mid = rest.astype(BF16)
    one_hot = pick.astype(BF16)
    wide_high = jnp.dot(w_high, one_hot, preferred_element_type=F32)
    wide_low = jnp.dot(w_mid, one_hot, preferred_element_type=F32)
    zero = jnp.zeros_like(wide_high)
    map_high = jnp.concatenate(
        [
            jnp.where(is_heat, zero, wide_high),
            jnp.where(is_heat, wide_high, zero),
            jnp.where(is_heat, deeper, zero),
        ],
        axis=0,
    ).astype(BF16)
    map_low = jnp.concatenate(
        [jnp.where(is_heat, zero, wide_low), jnp.where(is_heat, wide_low, zero), zero], axis=0
    ).astype(BF16)

    @pl.loop(0, n_lev - 1)
    def _(step):
        column_copy(step).wait()

    tiles = rows + rows // 2
    x = jnp.concatenate([recv[:, a].reshape(depth, 128) for a in range(tiles)], axis=1)
    x_high, x_low = halves(x)
    y = jnp.dot(map_high, x_high, preferred_element_type=F32)
    y += jnp.dot(map_high, x_low, preferred_element_type=F32)
    y += jnp.dot(map_low, x_high, preferred_element_type=F32)

    low_out = lax.broadcasted_iota(jnp.int32, (count, 128), 1) < 64

    def put(j, f, first, second):
        if f < 2:
            out[f, j, :, 0:128] = first
            out[f, j, :, 128:192] = second[:, 0:64]
        else:
            geo[j, :, 0:128] = first
            geo[j, :, 128:192] = second[:, 0:64]

    @pl.when(parity == 0)
    def _():
        for j in range(rows):
            for f in range(3):
                main = y[f * count : (f + 1) * count, j * 128 : (j + 1) * 128]
                at = (rows + j // 2) * 128
                side = y[f * count : (f + 1) * count, at : at + 128]
                if j % 2 == 1:
                    side = pltpu.roll(side, 64, 1)
                if f == 2:
                    main = main + surf[j : j + 1, 0:128]
                    side = side + surf[j : j + 1, 128:256]
                put(j, f, main, side)

    @pl.when(parity == 1)
    def _():
        for j in range(rows):
            for f in range(3):
                main = y[f * count : (f + 1) * count, j * 128 : (j + 1) * 128]
                at = (rows + j // 2) * 128
                side = y[f * count : (f + 1) * count, at : at + 128]
                if f == 2:
                    main = main + surf[j : j + 1, 256:384]
                    ground = surf[j : j + 1, 128:256]
                    side = side + (pltpu.roll(ground, 64, 1) if j % 2 == 0 else ground)
                if j % 2 == 1:
                    side = pltpu.roll(side, 64, 1)
                main = pltpu.roll(main, 64, 1)
                put(j, f, jnp.where(low_out, side, main), main)


def solution(mesh):
    n_lat, n_lev = mesh.shape["lat"], mesh.shape["lev"]

    def shards(fields, courant, cutoffs, surface, weights):
        _, rows, levs, length = fields.shape
        fwd, inv, turn = fourier_tables(length)
        count = weights.shape[0]
        tiles = rows + rows // 2
        any_spec = pl.BlockSpec(memory_space=pl.ANY)
        vmem_spec = pl.BlockSpec(memory_space=pltpu.VMEM)
        dma = pltpu.SemaphoreType.DMA
        return pl.pallas_call(
            functools.partial(kernel, n_lat, n_lev, 16 // rows),
            out_shape=(
                jax.ShapeDtypeStruct((2, rows, count, length // n_lev), F32),
                jax.ShapeDtypeStruct((rows, count, length // n_lev), F32),
            ),
            in_specs=[any_spec] * 8,
            out_specs=(vmem_spec, vmem_spec),
            scratch_shapes=[
                pltpu.VMEM(courant.shape, BF16),
                pltpu.SMEM(cutoffs.shape, jnp.int32),
                pltpu.VMEM((rows, 384), F32),
                pltpu.VMEM(weights.shape, F32),
                pltpu.VMEM(fwd.shape, BF16),
                pltpu.VMEM(inv.shape, BF16),
                pltpu.VMEM(turn.shape, F32),
                pltpu.VMEM((rows, 2 * levs, length), F32),
                pltpu.VMEM((rows, 2 * levs, length), F32),
                pltpu.VMEM((rows, 2 * levs, length), F32),
                pltpu.VMEM((rows + 1, 2 * levs, length), F32),
                pltpu.VMEM((2, 2, 2, 2 * levs, length), F32),
                pltpu.VMEM((2, levs, length), BF16),
                pltpu.VMEM((n_lev, tiles, 2 * levs, 128), F32),
                pltpu.VMEM((n_lev, tiles, 2 * levs, 128), F32),
                dma((9,)),
                dma((2, 2)),
                dma((2, 2)),
                dma((2,)),
                dma((2,)),
                dma((n_lev - 1,)),
                dma((n_lev - 1,)),
            ],
            compiler_params=pltpu.CompilerParams(collective_id=0, has_side_effects=True),
        )(fields, courant, cutoffs, surface, weights, fwd, inv, turn)

    return jax.shard_map(
        shards,
        mesh=mesh,
        in_specs=(
            P(None, "lat", "lev", None),
            P(None, "lat", "lev", None),
            P(),
            P("lat", None),
            P(),
        ),
        out_specs=(P(None, "lat", None, "lev"), P("lat", None, "lev")),
        check_vma=False,
    )
```

```python
import functools

import jax
import jax.numpy as jnp
import numpy as np
from jax import lax
from jax.experimental import pallas as pl
from jax.experimental.pallas import tpu as pltpu
from jax.sharding import PartitionSpec as P

MESH = pl.DeviceIdType.MESH
KMAX = 128
SEG = 256
CODE_MAX = 32767.0
STEPS = 256.0
ROUNDER = 1.5 * 2.0**23
F32 = jnp.float32
BF16 = jnp.bfloat16


def split_bf16(table):
    high = table.astype(np.float32).astype(jnp.bfloat16)
    low = (table - high.astype(np.float64)).astype(np.float32).astype(jnp.bfloat16)
    return np.stack([high, low])


def fourier_tables(length):
    waves = np.arange(KMAX)
    phase = (np.arange(SEG)[:, None] * waves[None, :]) % length
    angle = phase * (2.0 * np.pi / length)
    inner = np.concatenate([np.cos(angle), np.sin(angle)], axis=1)
    segments = length // SEG
    outer = (np.arange(segments)[:, None] * waves[None, :]) % segments
    outer = outer * (2.0 * np.pi / segments)
    turn = np.stack([np.cos(outer), np.sin(outer)], axis=1).astype(np.float32)
    return split_bf16(inner), split_bf16(inner.T), turn.reshape(2 * segments, KMAX)


def halves(x):
    high = x.astype(BF16)
    return high, (x - high.astype(F32)).astype(BF16)


def dot3(x, high, low):
    x_high, x_low = halves(x)
    out = jnp.dot(x_high, high, preferred_element_type=F32)
    out += jnp.dot(x_low, high, preferred_element_type=F32)
    return out + jnp.dot(x_high, low, preferred_element_type=F32)


def zonal(u, coef):
    length = u.shape[-1]
    pair = u + pltpu.roll(u, length - 1, 1)
    face = 8.0 * pair - (pltpu.roll(pair, 1, 1) + pltpu.roll(pair, length - 1, 1))
    flux = coef * face
    return u - (flux - pltpu.roll(flux, 1, 1))


def transport(
    n_lat, n_lev, polar,
    fields, courant, cutoffs, surface, weights, fwd, inv, turn,
    recv, maps, surf,
    cv, cut, wv, fwd_v, inv_v, turn_v,
    u, z, coef_x, coef_y, halo, halo_far, far_stage, cy_halo, send,
    in_sem, near_send, near_recv, far_send, far_recv, cy_send, cy_recv, a2a_send, a2a_recv,
    ring_one, ring_two,
):
    ilat, ilev = lax.axis_index("lat"), lax.axis_index("lev")
    rows, length = u.shape[0], u.shape[2]
    levs = u.shape[1] // 2
    segments = length // SEG
    n_y = n_lev // 2
    y, parity = lax.div(ilev, 2), lax.rem(ilev, 2)
    width = 3 * 128

    loads = [
        pltpu.make_async_copy(fields.at[0], u.at[:, 0:levs, :], in_sem.at[0]),
        pltpu.make_async_copy(fields.at[1], u.at[:, levs : 2 * levs, :], in_sem.at[1]),
        pltpu.make_async_copy(courant, cv, in_sem.at[2]),
        pltpu.make_async_copy(weights, wv, in_sem.at[5]),
        pltpu.make_async_copy(cutoffs, cut, in_sem.at[3]),
        pltpu.make_async_copy(
            surface.at[:, pl.ds(pl.multiple_of(y * width, 128), width)], surf, in_sem.at[4]
        ),
        pltpu.make_async_copy(fwd, fwd_v, in_sem.at[6]),
        pltpu.make_async_copy(inv, inv_v, in_sem.at[7]),
        pltpu.make_async_copy(turn, turn_v, in_sem.at[8]),
    ]

    has_minus, has_plus = ilat > 0, ilat < n_lat - 1
    barrier = pltpu.get_barrier_semaphore()

    def tell(sem, **where):
        pl.semaphore_signal(sem, inc=1, device_id=where, device_id_type=MESH)

    def level(step, core):
        return lax.rem(y + step + n_y, n_y) * 2 + core

    @pl.when(has_minus)
    def _():
        tell(barrier, lat=ilat - 1)

    @pl.when(has_plus)
    def _():
        tell(barrier, lat=ilat + 1)

    for core in range(2):
        tell(barrier, lev=level(1, core))
        tell(barrier, lev=level(-1, core))
    tell(barrier, lev=level(0, 1 - parity))

    for load in loads:
        load.start()

    neighbours = has_minus.astype(jnp.int32) + has_plus.astype(jnp.int32)
    pl.semaphore_wait(barrier, 5 + neighbours)

    def near_copy(phase, side, field):
        row = (rows - 1, 0)[side]
        half = slice(field * levs, (field + 1) * levs)
        source = fields.at[field, row] if phase == 0 else u.at[row, half, :]
        return pltpu.make_async_remote_copy(
            src_ref=source, dst_ref=halo.at[phase, side, half, :],
            send_sem=near_send.at[phase, side, field], recv_sem=near_recv.at[phase, side, field],
            device_id={"lat": ilat + (1, -1)[side]}, device_id_type=MESH,
        )

    def far_copy(phase, side):
        return pltpu.make_async_remote_copy(
            src_ref=far_stage.at[phase, side], dst_ref=halo_far.at[phase, side],
            send_sem=far_send.at[phase, side], recv_sem=far_recv.at[phase, side],
            device_id={"lat": ilat + (1, -1)[side]}, device_id_type=MESH,
        )

    def cy_copy(side):
        return pltpu.make_async_remote_copy(
            src_ref=courant.at[1, (rows - 1, 0)[side]], dst_ref=cy_halo.at[side],
            send_sem=cy_send.at[side], recv_sem=cy_recv.at[side],
            device_id={"lat": ilat + (1, -1)[side]}, device_id_type=MESH,
        )

    there = (has_plus, has_minus)

    def near_start(phase):
        for side in range(2):

            @pl.when(there[side])
            def _():
                near_copy(phase, side, 0).start()
                near_copy(phase, side, 1).start()
                if phase == 0:
                    cy_copy(side).start()

            @pl.when(jnp.logical_not(there[1 - side]))
            def _():
                halo[phase, side] = jnp.zeros(halo.shape[2:], F32)
                halo_far[phase, side] = jnp.zeros(halo_far.shape[2:], BF16)
                if phase == 0:
                    cy_halo[side] = jnp.zeros(cy_halo.shape[1:], BF16)

    def far_start(phase):
        for side in range(2):
            far_stage[phase, side] = u[(rows - 2, 1)[side]].astype(BF16)

            @pl.when(there[side])
            def _():
                far_copy(phase, side).start()

    def exchange_wait(phase):
        for side in range(2):

            @pl.when(there[1 - side])
            def _():
                near_copy(phase, side, 0).wait_recv()
                near_copy(phase, side, 1).wait_recv()
                far_copy(phase, side).wait_recv()
                if phase == 0:
                    cy_copy(side).wait_recv()

            @pl.when(there[side])
            def _():
                near_copy(phase, side, 0).wait_send()
                near_copy(phase, side, 1).wait_send()
                far_copy(phase, side).wait_send()
                if phase == 0:
                    cy_copy(side).wait_send()

    def both(x):
        return jnp.concatenate([x, x], axis=0)

    def cy_row(j):
        if j < 0:
            return both(cy_halo[0].astype(F32))
        if j >= rows:
            return both(cy_halo[1].astype(F32))
        return both(cv[1, j].astype(F32))

    def meridional(phase, start, piece):
        at = pl.ds(pl.multiple_of(start, 128), piece)
        full = [halo_far[phase, 0, :, at].astype(F32), halo[phase, 0, :, at]]
        full += [u[j, :, at] for j in range(rows)]
        full += [halo[phase, 1, :, at], halo_far[phase, 1, :, at].astype(F32)]
        before = None
        for face in range(rows + 1):
            a, b, d, e = full[face : face + 4]
            flux = coef_y[face, :, at] * (7.0 * (b + d) - (a + e))
            if before is not None:
                u[face - 1, :, at] = z[face - 1, :, at] - (flux - before)
            before = flux

    def low_pass():
        x = jnp.concatenate([u[j] for j in range(rows)], axis=0)
        count = x.shape[0]
        stacked = jnp.concatenate([x[:, q * SEG : (q + 1) * SEG] for q in range(segments)], axis=0)
        part = dot3(stacked, fwd_v[0], fwd_v[1])
        real = jnp.zeros((count, KMAX), F32)
        imag = jnp.zeros((count, KMAX), F32)
        for q in range(segments):
            p = part[q * count : (q + 1) * count, 0:KMAX]
            s = part[q * count : (q + 1) * count, KMAX : 2 * KMAX]
            c_q, s_q = turn_v[2 * q : 2 * q + 1, :], turn_v[2 * q + 1 : 2 * q + 2, :]
            real += c_q * p - s_q * s
            imag += s_q * p + c_q * s
        wave = lax.broadcasted_iota(jnp.int32, (2 * levs, KMAX), 1)
        double = jnp.where(wave == 0, 1.0 / length, 2.0 / length).astype(F32)
        weight = jnp.concatenate(
            [jnp.where(wave <= cut[ilat * rows + j], double, 0.0) for j in range(rows)], axis=0
        )
        real, imag = real * weight, imag * weight
        spread = []
        for q in range(segments):
            c_q, s_q = turn_v[2 * q : 2 * q + 1, :], turn_v[2 * q + 1 : 2 * q + 2, :]
            spread.append(
                jnp.concatenate([real * c_q + imag * s_q, imag * c_q - real * s_q], axis=1)
            )
        back = dot3(jnp.concatenate(spread, axis=0), inv_v[0], inv_v[1])
        for q in range(segments):
            for j in range(rows):
                at = q * count + j * 2 * levs
                u[j, :, q * SEG : (q + 1) * SEG] = back[at : at + 2 * levs]

    tiles = rows + rows // 2
    low_lane = lax.broadcasted_iota(jnp.int32, (2 * levs, 128), 1) < 64

    def encode(slot, parts):
        most = jnp.abs(parts[0])
        for part in parts[1:]:
            most = jnp.maximum(most, jnp.abs(part))
        power = jnp.ceil(jnp.log2(jnp.maximum(most, 1e-30)) * STEPS + 0.01)
        to_code = jnp.exp2(power * (-1.0 / STEPS)) * CODE_MAX
        for a, part in enumerate(parts):
            code = jnp.clip((part * to_code + ROUNDER) - ROUNDER, -CODE_MAX, CODE_MAX)
            send[slot, a] = code.astype(jnp.int32).astype(jnp.int16)
        send[slot, tiles] = power.astype(jnp.int32).astype(jnp.int16)

    def pack(e):
        def tile(j, t):
            return u[j, :, pl.ds(pl.multiple_of(e * width + t * 128, 128), 128)]

        first = [tile(j, 0) for j in range(rows)]
        second = [tile(j, 2) for j in range(rows)]
        for j in range(0, rows, 2):
            one, two = tile(j, 1), tile(j + 1, 1)
            first.append(jnp.where(low_lane, one, pltpu.roll(two, 64, 1)))
            second.append(jnp.where(low_lane, pltpu.roll(one, 64, 1), two))
        encode(2 * e, first)
        encode(2 * e + 1, second)

    def target(step):
        half = lax.div(step + 1, 2)
        return lax.rem(y + n_y // 2 + jnp.where(lax.rem(step, 2) == 1, -half, half), n_y)

    def column_copy(step, core):
        other = target(step) * 2 + core
        return pltpu.make_async_remote_copy(
            src_ref=send.at[other], dst_ref=recv.at[ilev],
            send_sem=a2a_send.at[step, core], recv_sem=a2a_recv.at[step, parity],
            device_id={"lev": other}, device_id_type=MESH,
        )

    def column_arrival(step, core):
        return pltpu.make_async_remote_copy(
            src_ref=send.at[0], dst_ref=recv.at[ilev],
            send_sem=a2a_send.at[step, core], recv_sem=a2a_recv.at[step, core],
            device_id={"lev": ilev}, device_id_type=MESH,
        )

    def columns(before):
        @pl.loop(0, n_y - 1)
        def _(step):
            e = target(step)
            before(e)
            pack(e)
            column_copy(step, 0).start()
            column_copy(step, 1).start()

        before(y)
        pack(y)
        column_copy(n_y - 1, 1 - parity).start()
        recv[ilev] = send[ilev]

    near_start(0)
    for load in loads[:2]:
        load.wait()
    far_start(0)
    tell(ring_one, lev=level(1, parity))
    tell(ring_one, lev=level(-1, parity))
    for load in loads[2:]:
        load.wait()
    for j in range(rows):
        cx = both(cv[0, j].astype(F32))
        coef_x[j] = (cx + pltpu.roll(cx, length - 1, 1)) * (1.0 / 24.0)
    for j in range(rows):
        z[j] = zonal(u[j], coef_x[j])
    for face in range(1, rows):
        coef_y[face] = (cy_row(face - 1) + cy_row(face)) * (1.0 / 24.0)
    exchange_wait(0)
    for face in (0, rows):
        coef_y[face] = (cy_row(face - 1) + cy_row(face)) * (1.0 / 24.0)
    is_polar = jnp.logical_or(ilat < polar, ilat >= n_lat - polar)

    @pl.loop(0, length // 512)
    def _(c):
        meridional(0, c * 512, 512)

    pl.when(is_polar)(low_pass)
    near_start(1)
    far_start(1)
    pl.semaphore_wait(ring_one, 2)
    tell(ring_two, lev=level(2, parity))
    tell(ring_two, lev=level(-2, parity))
    for j in range(rows):
        z[j] = zonal(u[j], coef_x[j])
    write_maps(n_lev, levs, wv, maps)
    pl.semaphore_wait(ring_two, 2)
    exchange_wait(1)

    @pl.when(is_polar)
    def _():
        @pl.loop(0, length // 512)
        def _(c):
            meridional(1, c * 512, 512)

        low_pass()
        columns(lambda e: None)

    @pl.when(jnp.logical_not(is_polar))
    def _():
        columns(lambda e: meridional(1, e * width, width))

    @pl.loop(0, n_y - 1)
    def _(step):
        for core in range(2):
            column_copy(step, core).wait_send()
            column_arrival(step, core).wait_recv()

    column_copy(n_y - 1, 1 - parity).wait_send()
    column_arrival(n_y - 1, 1 - parity).wait_recv()


def write_maps(n_lev, levs, wv, maps):
    count = n_lev * levs
    depth = n_lev * 2 * levs
    source = lax.broadcasted_iota(jnp.int32, (count, depth), 1)
    goal = lax.broadcasted_iota(jnp.int32, (count, depth), 0)
    level = lax.div(source, 2 * levs) * levs + lax.rem(source, levs)
    is_heat = lax.rem(source, 2 * levs) >= levs
    scale = count**-0.5
    deeper = jnp.where(level > goal, scale, jnp.where(level == goal, 0.5 * scale, 0.0))
    w_high, w_low = halves(wv[...])
    one_hot = (level == goal).astype(F32).astype(BF16)
    for half, w in enumerate((w_high, w_low)):
        wide = jnp.dot(w, one_hot, preferred_element_type=F32)
        maps[half, 0:count, :] = jnp.where(is_heat, 0.0, wide).astype(BF16)
        maps[half, count : 2 * count, :] = jnp.where(is_heat, wide, 0.0).astype(BF16)
    maps[0, 2 * count : 3 * count, :] = jnp.where(is_heat, deeper, 0.0).astype(BF16)
    maps[1, 2 * count : 3 * count, :] = jnp.zeros((count, depth), BF16)


def remap(recv, maps, surf, out, geo, out_v, geo_v, out_sem, geo_sem):
    n_lev, tiles, depth_rows = recv.shape[0], recv.shape[1] - 1, recv.shape[2]
    rows = surf.shape[0]
    count = maps.shape[1] // 3
    depth = n_lev * depth_rows
    parity = lax.rem(lax.axis_index("lev"), 2)
    scale = jnp.exp2(recv[:, tiles].astype(jnp.int32).astype(F32) * (1.0 / STEPS))
    scale = (scale * (1.0 / CODE_MAX)).reshape(depth, 128)
    values = [
        recv[:, a].astype(jnp.int32).astype(F32).reshape(depth, 128) * scale for a in range(tiles)
    ]
    x_high, x_low = halves(jnp.concatenate(values, axis=1))
    y = jnp.dot(maps[0], x_high, preferred_element_type=F32)
    y += jnp.dot(maps[0], x_low, preferred_element_type=F32)
    y += jnp.dot(maps[1], x_high, preferred_element_type=F32)
    low_out = lax.broadcasted_iota(jnp.int32, (count, 128), 1) < 64

    def put(j, f, first, second):
        if f < 2:
            out_v[f, j, :, 0:128] = first
            out_v[f, j, :, 128:192] = second[:, 0:64]
        else:
            geo_v[j, :, 0:128] = first
            geo_v[j, :, 128:192] = second[:, 0:64]

    @pl.when(parity == 0)
    def _():
        for j in range(rows):
            for f in range(3):
                main = y[f * count : (f + 1) * count, j * 128 : (j + 1) * 128]
                at = (rows + j // 2) * 128
                side = y[f * count : (f + 1) * count, at : at + 128]
                if j % 2 == 1:
                    side = pltpu.roll(side, 64, 1)
                if f == 2:
                    main = main + surf[j : j + 1, 0:128]
                    side = side + surf[j : j + 1, 128:256]
                put(j, f, main, side)

    @pl.when(parity == 1)
    def _():
        for j in range(rows):
            for f in range(3):
                main = y[f * count : (f + 1) * count, j * 128 : (j + 1) * 128]
                at = (rows + j // 2) * 128
                side = y[f * count : (f + 1) * count, at : at + 128]
                if f == 2:
                    main = main + surf[j : j + 1, 256:384]
                    ground = surf[j : j + 1, 128:256]
                    side = side + (pltpu.roll(ground, 64, 1) if j % 2 == 0 else ground)
                if j % 2 == 1:
                    side = pltpu.roll(side, 64, 1)
                main = pltpu.roll(main, 64, 1)
                put(j, f, jnp.where(low_out, side, main), main)

    for j in range(rows):
        copies = [pltpu.make_async_copy(out_v.at[f, j], out.at[f, j], out_sem.at[f, j]) for f in range(2)]
        copies.append(pltpu.make_async_copy(geo_v.at[j], geo.at[j], geo_sem.at[j]))
        for copy in copies:
            copy.start()
    for j in range(rows):
        for f in range(2):
            pltpu.make_async_copy(out_v.at[f, j], out.at[f, j], out_sem.at[f, j]).wait()
        pltpu.make_async_copy(geo_v.at[j], geo.at[j], geo_sem.at[j]).wait()


def solution(mesh):
    n_lat, n_lev = mesh.shape["lat"], mesh.shape["lev"]

    def shards(fields, courant, cutoffs, surface, weights):
        _, rows, levs, length = fields.shape
        fwd, inv, turn = fourier_tables(length)
        count = weights.shape[0]
        tiles = rows + rows // 2
        hbm_spec = pl.BlockSpec(memory_space=pltpu.HBM)
        vmem_spec = pl.BlockSpec(memory_space=pltpu.VMEM)
        dma = pltpu.SemaphoreType.DMA
        recv, maps, surf = pl.pallas_call(
            functools.partial(transport, n_lat, n_lev, 16 // rows),
            name="transport",
            out_shape=(
                pltpu.VMEM((n_lev, tiles + 1, 2 * levs, 128), jnp.int16),
                pltpu.VMEM((2, 3 * count, 2 * count), BF16),
                pltpu.VMEM((rows, 384), F32),
            ),
            in_specs=[hbm_spec] * 8,
            out_specs=(vmem_spec,) * 3,
            scratch_shapes=[
                pltpu.VMEM(courant.shape, BF16),
                pltpu.SMEM(cutoffs.shape, jnp.int32),
                pltpu.VMEM(weights.shape, F32),
                pltpu.VMEM(fwd.shape, BF16),
                pltpu.VMEM(inv.shape, BF16),
                pltpu.VMEM(turn.shape, F32),
                pltpu.VMEM((rows, 2 * levs, length), F32),
                pltpu.VMEM((rows, 2 * levs, length), F32),
                pltpu.VMEM((rows, 2 * levs, length), F32),
                pltpu.VMEM((rows + 1, 2 * levs, length), F32),
                pltpu.VMEM((2, 2, 2 * levs, length), F32),
                pltpu.VMEM((2, 2, 2 * levs, length), BF16),
                pltpu.VMEM((2, 2, 2 * levs, length), BF16),
                pltpu.VMEM((2, levs, length), BF16),
                pltpu.VMEM((n_lev, tiles + 1, 2 * levs, 128), jnp.int16),
                dma((9,)),
                dma((2, 2, 2)),
                dma((2, 2, 2)),
                dma((2, 2)),
                dma((2, 2)),
                dma((2,)),
                dma((2,)),
                dma((n_lev // 2, 2)),
                dma((n_lev // 2, 2)),
                pltpu.SemaphoreType.REGULAR,
                pltpu.SemaphoreType.REGULAR,
            ],
            compiler_params=pltpu.CompilerParams(
                collective_id=0, has_side_effects=True
            ),
        )(fields, courant, cutoffs, surface, weights, fwd, inv, turn)
        columns = length // n_lev
        return pl.pallas_call(
            remap,
            name="remap",
            out_shape=(
                jax.ShapeDtypeStruct((2, rows, count, columns), F32),
                jax.ShapeDtypeStruct((rows, count, columns), F32),
            ),
            in_specs=[vmem_spec] * 3,
            out_specs=(hbm_spec, hbm_spec),
            scratch_shapes=[
                pltpu.VMEM((2, rows, count, columns), F32),
                pltpu.VMEM((rows, count, columns), F32),
                dma((2, rows)),
                dma((rows,)),
            ],
            compiler_params=pltpu.CompilerParams(vmem_limit_bytes=24 << 20),
        )(recv, maps, surf)

    return jax.shard_map(
        shards,
        mesh=mesh,
        in_specs=(
            P(None, "lat", "lev", None),
            P(None, "lat", "lev", None),
            P(),
            P("lat", None),
            P(),
        ),
        out_specs=(P(None, "lat", None, "lev"), P("lat", None, "lev")),
        check_vma=False,
    )
```

```python
import functools

import jax
import jax.numpy as jnp
import numpy as np
from jax import lax
from jax.experimental import pallas as pl
from jax.experimental.pallas import tpu as pltpu
from jax.sharding import PartitionSpec as P

MESH = pl.DeviceIdType.MESH
KMAX = 128
SEG = 256
CODE_MAX = 32767.0
STEPS = 256.0
ROUNDER = 1.5 * 2.0**23
F32 = jnp.float32
BF16 = jnp.bfloat16


def split_bf16(table):
    high = table.astype(np.float32).astype(jnp.bfloat16)
    low = (table - high.astype(np.float64)).astype(np.float32).astype(jnp.bfloat16)
    return np.stack([high, low])


def fourier_tables(length):
    waves = np.arange(KMAX)
    phase = (np.arange(SEG)[:, None] * waves[None, :]) % length
    angle = phase * (2.0 * np.pi / length)
    inner = np.concatenate([np.cos(angle), np.sin(angle)], axis=1)
    segments = length // SEG
    outer = (np.arange(segments)[:, None] * waves[None, :]) % segments
    outer = outer * (2.0 * np.pi / segments)
    turn = np.stack([np.cos(outer), np.sin(outer)], axis=1).astype(np.float32)
    return split_bf16(inner), split_bf16(inner.T), turn.reshape(2 * segments, KMAX)


def halves(x):
    high = x.astype(BF16)
    return high, (x - high.astype(F32)).astype(BF16)


def dot3(x, high, low):
    x_high, x_low = halves(x)
    out = jnp.dot(x_high, high, preferred_element_type=F32)
    out += jnp.dot(x_low, high, preferred_element_type=F32)
    return out + jnp.dot(x_high, low, preferred_element_type=F32)


def zonal(u, coef):
    length = u.shape[-1]
    pair = u + pltpu.roll(u, length - 1, 1)
    face = 8.0 * pair - (pltpu.roll(pair, 1, 1) + pltpu.roll(pair, length - 1, 1))
    flux = coef * face
    return u - (flux - pltpu.roll(flux, 1, 1))


def transport(
    n_lat, n_lev, polar,
    fields, courant, cutoffs, surface, weights, fwd, inv, turn,
    recv, maps, surf,
    cv, cut, wv, fwd_v, inv_v, turn_v,
    u, v, z, coef_x, coef_y, near, far, far_stage, cx_halo, cy_halo, send,
    in_sem, halo_send, halo_recv, a2a_send, a2a_recv,
    ring_one, ring_two,
):
    ilat, ilev = lax.axis_index("lat"), lax.axis_index("lev")
    rows, length = u.shape[0], u.shape[2]
    levs = u.shape[1] // 2
    segments = length // SEG
    n_y = n_lev // 2
    y, parity = lax.div(ilev, 2), lax.rem(ilev, 2)
    width = 3 * 128

    loads = [
        pltpu.make_async_copy(fields.at[0], u.at[:, 0:levs, :], in_sem.at[0]),
        pltpu.make_async_copy(fields.at[1], u.at[:, levs : 2 * levs, :], in_sem.at[1]),
        pltpu.make_async_copy(courant, cv, in_sem.at[2]),
        pltpu.make_async_copy(weights, wv, in_sem.at[5]),
        pltpu.make_async_copy(cutoffs, cut, in_sem.at[3]),
        pltpu.make_async_copy(
            surface.at[:, pl.ds(pl.multiple_of(y * width, 128), width)], surf, in_sem.at[4]
        ),
        pltpu.make_async_copy(fwd, fwd_v, in_sem.at[6]),
        pltpu.make_async_copy(inv, inv_v, in_sem.at[7]),
        pltpu.make_async_copy(turn, turn_v, in_sem.at[8]),
    ]

    has_minus, has_plus = ilat > 0, ilat < n_lat - 1
    barrier = pltpu.get_barrier_semaphore()

    def tell(sem, **where):
        pl.semaphore_signal(sem, inc=1, device_id=where, device_id_type=MESH)

    def level(step, core):
        return lax.rem(y + step + n_y, n_y) * 2 + core

    @pl.when(has_minus)
    def _():
        tell(barrier, lat=ilat - 1)

    @pl.when(has_plus)
    def _():
        tell(barrier, lat=ilat + 1)

    for core in range(2):
        tell(barrier, lev=level(1, core))
        tell(barrier, lev=level(-1, core))
    tell(barrier, lev=level(0, 1 - parity))

    for load in loads[:3]:
        load.start()

    neighbours = has_minus.astype(jnp.int32) + has_plus.astype(jnp.int32)
    pl.semaphore_wait(barrier, 5 + neighbours)

    def halo_copies(side):
        row = (rows - 1, 0)[side]
        pieces = [
            (fields.at[0, row], near.at[side, 0:levs, :]),
            (fields.at[1, row], near.at[side, levs : 2 * levs, :]),
            (courant.at[1, pl.ds((1, 0)[side], 3)], cy_halo.at[side]),
            (courant.at[0, pl.ds((2, 0)[side], 2)], cx_halo.at[side]),
            (far_stage.at[pl.ds((0, 1)[side], 3)], far.at[side]),
        ]
        return [
            pltpu.make_async_remote_copy(
                src_ref=source, dst_ref=goal,
                send_sem=halo_send.at[side, n], recv_sem=halo_recv.at[side, n],
                device_id={"lat": ilat + (1, -1)[side]}, device_id_type=MESH,
            )
            for n, (source, goal) in enumerate(pieces)
        ]

    there = (has_plus, has_minus)

    def halo_start(first, last):
        for side in (0, 1):

            @pl.when(there[side])
            def _():
                for copy in halo_copies(side)[first:last]:
                    copy.start()

    def halo_wait(side):
        @pl.when(there[1 - side])
        def _():
            for copy in halo_copies(side):
                copy.wait_recv()

        @pl.when(jnp.logical_not(there[1 - side]))
        def _():
            near[side] = jnp.zeros(near.shape[1:], F32)
            far[side] = jnp.zeros(far.shape[1:], BF16)
            cx_halo[side] = jnp.zeros(cx_halo.shape[1:], BF16)
            cy_halo[side] = jnp.zeros(cy_halo.shape[1:], BF16)

    def both(x):
        return jnp.concatenate([x, x], axis=0)

    def cy_row(r):
        if r < 0:
            return both(cy_halo[0, r + 3].astype(F32))
        if r >= rows:
            return both(cy_halo[1, r - rows].astype(F32))
        return both(cv[1, r].astype(F32))

    def cx_row(r):
        if r < 0:
            return both(cx_halo[0, r + 2].astype(F32))
        if r >= rows:
            return both(cx_halo[1, r - rows].astype(F32))
        return both(cv[0, r].astype(F32))

    def u_row(r, at=slice(None)):
        if r == -1:
            return near[0, :, at]
        if r < 0:
            return far[0, r + 4, :, at].astype(F32)
        if r == rows:
            return near[1, :, at]
        if r > rows:
            return far[1, r - rows - 1, :, at].astype(F32)
        return u[r, :, at]

    def v_row(r, at=slice(None)):
        return v[r + 2, :, at]

    def set_coef_x(r):
        cx = cx_row(r)
        coef_x[r + 2] = (cx + pltpu.roll(cx, length - 1, 1)) * (1.0 / 24.0)

    def set_coef_y(r):
        coef_y[r + 3] = (cy_row(r) + cy_row(r + 1)) * (1.0 / 24.0)

    def meridional(source, goal, shift, first, count, start, piece):
        at = pl.ds(pl.multiple_of(start, 128), piece)
        full = [source(r, at) for r in range(first - 2, first + count + 2)]
        before = None
        for n in range(count + 1):
            a, b, d, e = full[n : n + 4]
            r = first + n - 1
            flux = coef_y[r + 3, :, at] * (7.0 * (b + d) - (a + e))
            if before is not None:
                goal[r + shift, :, at] = z[r + 2, :, at] - (flux - before)
            before = flux

    def first_substep(side):
        half = rows // 2
        if side == 0:
            group, outer, faces, other = -2, (-2, -1), (-3, -2, -1), ilat - 1
        else:
            group, outer, other = half, (rows, rows + 1), ilat + 1
            faces = (rows - 1, rows, rows + 1)
        for r in faces:
            set_coef_y(r)
        for r in outer:
            set_coef_x(r)
            z[r + 2] = zonal(u_row(r), coef_x[r + 2])

        @pl.loop(0, length // 512)
        def _(c):
            meridional(u_row, v, 2, group, rows, c * 512, 512)

        @pl.when(jnp.logical_not(there[1 - side]))
        def _():
            for r in outer:
                v[r + 2] = jnp.zeros(v.shape[1:], F32)

        def band_is_polar(band):
            return jnp.logical_or(band < polar, band >= n_lat - polar)

        @pl.when(jnp.logical_or(band_is_polar(ilat), band_is_polar(other)))
        def _():
            low_pass(v, group + 2, group)

        for r in range(max(group, 0), min(group + rows, rows)):
            z[r + 2] = zonal(v_row(r), coef_x[r + 2])

    def low_pass(ref, base, first):
        x = jnp.concatenate([ref[base + j] for j in range(rows)], axis=0)
        cuts = [cut[jnp.clip(ilat * rows + first + j, 0, n_lat * rows - 1)] for j in range(rows)]
        count = x.shape[0]
        stacked = jnp.concatenate([x[:, q * SEG : (q + 1) * SEG] for q in range(segments)], axis=0)
        part = dot3(stacked, fwd_v[0], fwd_v[1])
        real = jnp.zeros((count, KMAX), F32)
        imag = jnp.zeros((count, KMAX), F32)
        for q in range(segments):
            p = part[q * count : (q + 1) * count, 0:KMAX]
            s = part[q * count : (q + 1) * count, KMAX : 2 * KMAX]
            c_q, s_q = turn_v[2 * q : 2 * q + 1, :], turn_v[2 * q + 1 : 2 * q + 2, :]
            real += c_q * p - s_q * s
            imag += s_q * p + c_q * s
        wave = lax.broadcasted_iota(jnp.int32, (2 * levs, KMAX), 1)
        double = jnp.where(wave == 0, 1.0 / length, 2.0 / length).astype(F32)
        weight = jnp.concatenate(
            [jnp.where(wave <= cuts[j], double, 0.0) for j in range(rows)], axis=0
        )
        real, imag = real * weight, imag * weight
        spread = []
        for q in range(segments):
            c_q, s_q = turn_v[2 * q : 2 * q + 1, :], turn_v[2 * q + 1 : 2 * q + 2, :]
            spread.append(
                jnp.concatenate([real * c_q + imag * s_q, imag * c_q - real * s_q], axis=1)
            )
        back = dot3(jnp.concatenate(spread, axis=0), inv_v[0], inv_v[1])
        for q in range(segments):
            for j in range(rows):
                at = q * count + j * 2 * levs
                piece = slice(q * SEG, (q + 1) * SEG)
                ref[base + j, :, piece] = jnp.where(
                    cuts[j] < length // 2, back[at : at + 2 * levs], ref[base + j, :, piece]
                )

    tiles = rows + rows // 2
    low_lane = lax.broadcasted_iota(jnp.int32, (2 * levs, 128), 1) < 64

    def encode(slot, parts):
        most = jnp.abs(parts[0])
        for part in parts[1:]:
            most = jnp.maximum(most, jnp.abs(part))
        power = jnp.ceil(jnp.log2(jnp.maximum(most, 1e-30)) * STEPS + 0.01)
        to_code = jnp.exp2(power * (-1.0 / STEPS)) * CODE_MAX
        for a, part in enumerate(parts):
            code = jnp.clip((part * to_code + ROUNDER) - ROUNDER, -CODE_MAX, CODE_MAX)
            send[slot, a] = code.astype(jnp.int32).astype(jnp.int16)
        send[slot, tiles] = power.astype(jnp.int32).astype(jnp.int16)

    def pack(e):
        def tile(j, t):
            return u[j, :, pl.ds(pl.multiple_of(e * width + t * 128, 128), 128)]

        first = [tile(j, 0) for j in range(rows)]
        second = [tile(j, 2) for j in range(rows)]
        for j in range(0, rows, 2):
            one, two = tile(j, 1), tile(j + 1, 1)
            first.append(jnp.where(low_lane, one, pltpu.roll(two, 64, 1)))
            second.append(jnp.where(low_lane, pltpu.roll(one, 64, 1), two))
        encode(2 * e, first)
        encode(2 * e + 1, second)

    def target(step):
        half = lax.div(step + 1, 2)
        return lax.rem(y + n_y // 2 + jnp.where(lax.rem(step, 2) == 1, -half, half), n_y)

    def column_copy(step, core):
        other = target(step) * 2 + core
        return pltpu.make_async_remote_copy(
            src_ref=send.at[other], dst_ref=recv.at[ilev],
            send_sem=a2a_send.at[step, core], recv_sem=a2a_recv.at[step, parity],
            device_id={"lev": other}, device_id_type=MESH,
        )

    def column_arrival(step, core):
        return pltpu.make_async_remote_copy(
            src_ref=send.at[0], dst_ref=recv.at[ilev],
            send_sem=a2a_send.at[step, core], recv_sem=a2a_recv.at[step, core],
            device_id={"lev": ilev}, device_id_type=MESH,
        )

    def columns(before):
        @pl.loop(0, n_y - 1)
        def _(step):
            e = target(step)
            before(e)
            pack(e)
            column_copy(step, 0).start()
            column_copy(step, 1).start()

        before(y)
        pack(y)
        column_copy(n_y - 1, 1 - parity).start()
        recv[ilev] = send[ilev]

    halo_start(0, 4)
    for load in loads[3:]:
        load.start()
    for load in loads[:2]:
        load.wait()
    for r in range(rows):
        far_stage[r] = u[r].astype(BF16)
    halo_start(4, 5)
    tell(ring_one, lev=level(1, parity))
    tell(ring_one, lev=level(-1, parity))
    for load in loads[2:]:
        load.wait()
    for r in range(rows):
        set_coef_x(r)
        z[r + 2] = zonal(u[r], coef_x[r + 2])
    for r in range(rows - 1):
        set_coef_y(r)
    write_maps(n_lev, levs, wv, maps)
    halo_wait(1)
    first_substep(1)
    pl.semaphore_wait(ring_one, 2)
    tell(ring_two, lev=level(2, parity))
    tell(ring_two, lev=level(-2, parity))
    halo_wait(0)
    first_substep(0)
    pl.semaphore_wait(ring_two, 2)
    is_polar = jnp.logical_or(ilat < polar, ilat >= n_lat - polar)

    @pl.when(is_polar)
    def _():
        @pl.loop(0, length // 512)
        def _(c):
            meridional(v_row, u, 0, 0, rows, c * 512, 512)

        low_pass(u, 0, 0)
        columns(lambda e: None)

    @pl.when(jnp.logical_not(is_polar))
    def _():
        columns(lambda e: meridional(v_row, u, 0, 0, rows, e * width, width))

    for side in (0, 1):

        @pl.when(there[side])
        def _():
            for copy in halo_copies(side):
                copy.wait_send()

    @pl.loop(0, n_y - 1)
    def _(step):
        for core in range(2):
            column_copy(step, core).wait_send()
            column_arrival(step, core).wait_recv()

    column_copy(n_y - 1, 1 - parity).wait_send()
    column_arrival(n_y - 1, 1 - parity).wait_recv()


def write_maps(n_lev, levs, wv, maps):
    count = n_lev * levs
    depth = n_lev * 2 * levs
    source = lax.broadcasted_iota(jnp.int32, (count, depth), 1)
    goal = lax.broadcasted_iota(jnp.int32, (count, depth), 0)
    level = lax.div(source, 2 * levs) * levs + lax.rem(source, levs)
    is_heat = lax.rem(source, 2 * levs) >= levs
    scale = count**-0.5
    deeper = jnp.where(level > goal, scale, jnp.where(level == goal, 0.5 * scale, 0.0))
    w_high, w_low = halves(wv[...])
    one_hot = (level == goal).astype(F32).astype(BF16)
    for half, w in enumerate((w_high, w_low)):
        wide = jnp.dot(w, one_hot, preferred_element_type=F32)
        maps[half, 0:count, :] = jnp.where(is_heat, 0.0, wide).astype(BF16)
        maps[half, count : 2 * count, :] = jnp.where(is_heat, wide, 0.0).astype(BF16)
    maps[0, 2 * count : 3 * count, :] = jnp.where(is_heat, deeper, 0.0).astype(BF16)
    maps[1, 2 * count : 3 * count, :] = jnp.zeros((count, depth), BF16)


def remap(recv, maps, surf, out, geo, out_v, geo_v, out_sem, geo_sem):
    n_lev, tiles, depth_rows = recv.shape[0], recv.shape[1] - 1, recv.shape[2]
    rows = surf.shape[0]
    count = maps.shape[1] // 3
    depth = n_lev * depth_rows
    parity = lax.rem(lax.axis_index("lev"), 2)
    scale = jnp.exp2(recv[:, tiles].astype(jnp.int32).astype(F32) * (1.0 / STEPS))
    scale = (scale * (1.0 / CODE_MAX)).reshape(depth, 128)
    values = [
        recv[:, a].astype(jnp.int32).astype(F32).reshape(depth, 128) * scale for a in range(tiles)
    ]
    x_high, x_low = halves(jnp.concatenate(values, axis=1))
    y = jnp.dot(maps[0], x_high, preferred_element_type=F32)
    y += jnp.dot(maps[0], x_low, preferred_element_type=F32)
    y += jnp.dot(maps[1], x_high, preferred_element_type=F32)
    low_out = lax.broadcasted_iota(jnp.int32, (count, 128), 1) < 64

    def put(j, f, first, second):
        if f < 2:
            out_v[f, j, :, 0:128] = first
            out_v[f, j, :, 128:192] = second[:, 0:64]
        else:
            geo_v[j, :, 0:128] = first
            geo_v[j, :, 128:192] = second[:, 0:64]

    @pl.when(parity == 0)
    def _():
        for j in range(rows):
            for f in range(3):
                main = y[f * count : (f + 1) * count, j * 128 : (j + 1) * 128]
                at = (rows + j // 2) * 128
                side = y[f * count : (f + 1) * count, at : at + 128]
                if j % 2 == 1:
                    side = pltpu.roll(side, 64, 1)
                if f == 2:
                    main = main + surf[j : j + 1, 0:128]
                    side = side + surf[j : j + 1, 128:256]
                put(j, f, main, side)

    @pl.when(parity == 1)
    def _():
        for j in range(rows):
            for f in range(3):
                main = y[f * count : (f + 1) * count, j * 128 : (j + 1) * 128]
                at = (rows + j // 2) * 128
                side = y[f * count : (f + 1) * count, at : at + 128]
                if f == 2:
                    main = main + surf[j : j + 1, 256:384]
                    ground = surf[j : j + 1, 128:256]
                    side = side + (pltpu.roll(ground, 64, 1) if j % 2 == 0 else ground)
                if j % 2 == 1:
                    side = pltpu.roll(side, 64, 1)
                main = pltpu.roll(main, 64, 1)
                put(j, f, jnp.where(low_out, side, main), main)

    for j in range(rows):
        copies = [pltpu.make_async_copy(out_v.at[f, j], out.at[f, j], out_sem.at[f, j]) for f in range(2)]
        copies.append(pltpu.make_async_copy(geo_v.at[j], geo.at[j], geo_sem.at[j]))
        for copy in copies:
            copy.start()
    for j in range(rows):
        for f in range(2):
            pltpu.make_async_copy(out_v.at[f, j], out.at[f, j], out_sem.at[f, j]).wait()
        pltpu.make_async_copy(geo_v.at[j], geo.at[j], geo_sem.at[j]).wait()


def solution(mesh):
    n_lat, n_lev = mesh.shape["lat"], mesh.shape["lev"]

    def shards(fields, courant, cutoffs, surface, weights):
        _, rows, levs, length = fields.shape
        fwd, inv, turn = fourier_tables(length)
        count = weights.shape[0]
        tiles = rows + rows // 2
        hbm_spec = pl.BlockSpec(memory_space=pltpu.HBM)
        vmem_spec = pl.BlockSpec(memory_space=pltpu.VMEM)
        dma = pltpu.SemaphoreType.DMA
        recv, maps, surf = pl.pallas_call(
            functools.partial(transport, n_lat, n_lev, 16 // rows),
            name="transport",
            out_shape=(
                pltpu.VMEM((n_lev, tiles + 1, 2 * levs, 128), jnp.int16),
                pltpu.VMEM((2, 3 * count, 2 * count), BF16),
                pltpu.VMEM((rows, 384), F32),
            ),
            in_specs=[hbm_spec] * 8,
            out_specs=(vmem_spec,) * 3,
            scratch_shapes=[
                pltpu.VMEM(courant.shape, BF16),
                pltpu.SMEM(cutoffs.shape, jnp.int32),
                pltpu.VMEM(weights.shape, F32),
                pltpu.VMEM(fwd.shape, BF16),
                pltpu.VMEM(inv.shape, BF16),
                pltpu.VMEM(turn.shape, F32),
                pltpu.VMEM((rows, 2 * levs, length), F32),
                pltpu.VMEM((rows + 4, 2 * levs, length), F32),
                pltpu.VMEM((rows + 4, 2 * levs, length), F32),
                pltpu.VMEM((rows + 4, 2 * levs, length), F32),
                pltpu.VMEM((rows + 5, 2 * levs, length), F32),
                pltpu.VMEM((2, 2 * levs, length), F32),
                pltpu.VMEM((2, 3, 2 * levs, length), BF16),
                pltpu.VMEM((rows, 2 * levs, length), BF16),
                pltpu.VMEM((2, 2, levs, length), BF16),
                pltpu.VMEM((2, 3, levs, length), BF16),
                pltpu.VMEM((n_lev, tiles + 1, 2 * levs, 128), jnp.int16),
                dma((9,)),
                dma((2, 5)),
                dma((2, 5)),
                dma((n_lev // 2, 2)),
                dma((n_lev // 2, 2)),
                pltpu.SemaphoreType.REGULAR,
                pltpu.SemaphoreType.REGULAR,
            ],
            compiler_params=pltpu.CompilerParams(
                collective_id=0, has_side_effects=True
            ),
        )(fields, courant, cutoffs, surface, weights, fwd, inv, turn)
        columns = length // n_lev
        return pl.pallas_call(
            remap,
            name="remap",
            out_shape=(
                jax.ShapeDtypeStruct((2, rows, count, columns), F32),
                jax.ShapeDtypeStruct((rows, count, columns), F32),
            ),
            in_specs=[vmem_spec] * 3,
            out_specs=(hbm_spec, hbm_spec),
            scratch_shapes=[
                pltpu.VMEM((2, rows, count, columns), F32),
                pltpu.VMEM((rows, count, columns), F32),
                dma((2, rows)),
                dma((rows,)),
            ],
            compiler_params=pltpu.CompilerParams(vmem_limit_bytes=24 << 20),
        )(recv, maps, surf)

    return jax.shard_map(
        shards,
        mesh=mesh,
        in_specs=(
            P(None, "lat", "lev", None),
            P(None, "lat", "lev", None),
            P(),
            P("lat", None),
            P(),
        ),
        out_specs=(P(None, "lat", None, "lev"), P("lat", None, "lev")),
        check_vma=False,
    )
```

```python
import functools

import jax
import jax.numpy as jnp
import numpy as np
from jax import lax
from jax.experimental import pallas as pl
from jax.experimental.pallas import tpu as pltpu
from jax.sharding import PartitionSpec as P

MESH = pl.DeviceIdType.MESH
KMAX = 128
SEG = 256
CODE_MAX = 32767.0
STEPS = 256.0
ROUNDER = 1.5 * 2.0**23
F32 = jnp.float32
BF16 = jnp.bfloat16


def split_bf16(table):
    high = table.astype(np.float32).astype(jnp.bfloat16)
    low = (table - high.astype(np.float64)).astype(np.float32).astype(jnp.bfloat16)
    return np.stack([high, low])


def fourier_tables(length):
    waves = np.arange(KMAX)
    phase = (np.arange(SEG)[:, None] * waves[None, :]) % length
    angle = phase * (2.0 * np.pi / length)
    inner = np.concatenate([np.cos(angle), np.sin(angle)], axis=1)
    segments = length // SEG
    outer = (np.arange(segments)[:, None] * waves[None, :]) % segments
    outer = outer * (2.0 * np.pi / segments)
    turn = np.stack([np.cos(outer), np.sin(outer)], axis=1).astype(np.float32)
    return split_bf16(inner), split_bf16(inner.T), turn.reshape(2 * segments, KMAX)


def halves(x):
    high = x.astype(BF16)
    return high, (x - high.astype(F32)).astype(BF16)


def dot3(x, high, low):
    x_high, x_low = halves(x)
    out = jnp.dot(x_high, high, preferred_element_type=F32)
    out += jnp.dot(x_low, high, preferred_element_type=F32)
    return out + jnp.dot(x_high, low, preferred_element_type=F32)


def zonal(u, coef):
    length = u.shape[-1]
    pair = u + pltpu.roll(u, length - 1, 1)
    face = 8.0 * pair - (pltpu.roll(pair, 1, 1) + pltpu.roll(pair, length - 1, 1))
    flux = coef * face
    return u - (flux - pltpu.roll(flux, 1, 1))


def transport(
    n_lat, n_lev, polar,
    fields, courant, cutoffs, surface, weights, fwd, inv, turn,
    recv, maps, surf,
    cv, cut, wv, fwd_v, inv_v, turn_v,
    u, v, z, coef_x, coef_y, near, far, stage, cy_halo, send,
    in_sem, halo_send, halo_recv, a2a_send, a2a_recv,
    ring_one, ring_two,
):
    ilat, ilev = lax.axis_index("lat"), lax.axis_index("lev")
    rows, length = u.shape[0], u.shape[2]
    levs = u.shape[1] // 2
    segments = length // SEG
    n_y = n_lev // 2
    y, parity = lax.div(ilev, 2), lax.rem(ilev, 2)
    width = 3 * 128

    loads = [
        pltpu.make_async_copy(fields.at[0], u.at[:, 0:levs, :], in_sem.at[0]),
        pltpu.make_async_copy(fields.at[1], u.at[:, levs : 2 * levs, :], in_sem.at[1]),
        pltpu.make_async_copy(courant, cv, in_sem.at[2]),
        pltpu.make_async_copy(weights, wv, in_sem.at[5]),
        pltpu.make_async_copy(cutoffs, cut, in_sem.at[3]),
        pltpu.make_async_copy(
            surface.at[:, pl.ds(pl.multiple_of(y * width, 128), width)], surf, in_sem.at[4]
        ),
        pltpu.make_async_copy(fwd, fwd_v, in_sem.at[6]),
        pltpu.make_async_copy(inv, inv_v, in_sem.at[7]),
        pltpu.make_async_copy(turn, turn_v, in_sem.at[8]),
    ]

    has_minus, has_plus = ilat > 0, ilat < n_lat - 1
    barrier = pltpu.get_barrier_semaphore()

    def tell(sem, **where):
        pl.semaphore_signal(sem, inc=1, device_id=where, device_id_type=MESH)

    def level(step, core):
        return lax.rem(y + step + n_y, n_y) * 2 + core

    @pl.when(has_minus)
    def _():
        tell(barrier, lat=ilat - 1)

    @pl.when(has_plus)
    def _():
        tell(barrier, lat=ilat + 1)

    for core in range(2):
        tell(barrier, lev=level(1, core))
        tell(barrier, lev=level(-1, core))
    tell(barrier, lev=level(0, 1 - parity))

    for load in loads[:3]:
        load.start()

    neighbours = has_minus.astype(jnp.int32) + has_plus.astype(jnp.int32)
    pl.semaphore_wait(barrier, 5 + neighbours)

    def halo_copies(side):
        row = (rows - 1, 0)[side]
        pieces = [
            (fields.at[0, row], near.at[side, 0:levs, :]),
            (fields.at[1, row], near.at[side, levs : 2 * levs, :]),
            (courant.at[1, pl.ds((rows - 2, 0)[side], 2)], cy_halo.at[side]),
            (stage.at[side, 0], far.at[side, 0]),
            (stage.at[side, pl.ds(1, 2)], far.at[side, pl.ds(1, 2)]),
        ]
        return [
            pltpu.make_async_remote_copy(
                src_ref=source, dst_ref=goal,
                send_sem=halo_send.at[side, n], recv_sem=halo_recv.at[side, n],
                device_id={"lat": ilat + (1, -1)[side]}, device_id_type=MESH,
            )
            for n, (source, goal) in enumerate(pieces)
        ]

    there = (has_plus, has_minus)

    def halo_start(first, last):
        for side in (0, 1):

            @pl.when(there[side])
            def _():
                for copy in halo_copies(side)[first:last]:
                    copy.start()

    def halo_wait(side):
        @pl.when(there[1 - side])
        def _():
            for copy in halo_copies(side):
                copy.wait_recv()

        @pl.when(jnp.logical_not(there[1 - side]))
        def _():
            near[side] = jnp.zeros(near.shape[1:], F32)
            far[side] = jnp.zeros(far.shape[1:], BF16)
            cy_halo[side] = jnp.zeros(cy_halo.shape[1:], BF16)

    def both(x):
        return jnp.concatenate([x, x], axis=0)

    def cy_row(r):
        if r < 0:
            return both(cy_halo[0, r + 2].astype(F32))
        if r >= rows:
            return both(cy_halo[1, r - rows].astype(F32))
        return both(cv[1, r].astype(F32))

    def v_row(r, at=slice(None)):
        return v[r + 2, :, at]

    def set_coef_x(r):
        cx = both(cv[0, r].astype(F32))
        coef_x[r] = (cx + pltpu.roll(cx, length - 1, 1)) * (1.0 / 24.0)

    def set_coef_y(r):
        coef_y[r + 2] = (cy_row(r) + cy_row(r + 1)) * (1.0 / 24.0)

    def pieces(body, piece=512):
        @pl.loop(0, length // piece)
        def _(c):
            body(pl.ds(pl.multiple_of(c * piece, 128), piece))

    def own_part(at):
        u0, u1, u2, u3 = (u[r, :, at] for r in range(4))
        low = coef_y[2, :, at] * (7.0 * (u0 + u1) - u2)
        middle = coef_y[3, :, at] * (7.0 * (u1 + u2) - (u0 + u3))
        high = coef_y[4, :, at] * (7.0 * (u2 + u3) - u1)
        z0, z1 = z[0, :, at] - low, z[1, :, at] - middle + low
        z2, z3 = z[2, :, at] - high + middle, z[3, :, at] + high
        z[0, :, at], z[1, :, at], z[2, :, at], z[3, :, at] = z0, z1, z2, z3
        stage[0, 1, :, at] = (z3 - u3).astype(BF16)
        stage[0, 2, :, at] = z2.astype(BF16)
        stage[1, 1, :, at] = (z0 - u0).astype(BF16)
        stage[1, 2, :, at] = z1.astype(BF16)

    def halo_part(side, at):
        edge, inner, sign = ((0, 1, 1.0), (rows - 1, rows - 2, -1.0))[side]
        outer, outermost = ((1, 0), (rows + 2, rows + 3))[side]
        beyond, shared, inside = ((0, 1, 2), (rows + 2, rows + 1, rows))[side]
        n, f = near[side, :, at], far[side, 0, :, at].astype(F32)
        change, value = far[side, 1, :, at].astype(F32), far[side, 2, :, at].astype(F32)
        flux = coef_y[shared, :, at] * (7.0 * (n + u[edge, :, at]) - (f + u[inner, :, at]))
        mine = coef_y[inside, :, at] * n
        theirs = coef_y[beyond, :, at] * u[edge, :, at]
        v[edge + 2, :, at] = z[edge, :, at] + sign * (mine + flux)
        v[inner + 2, :, at] = z[inner, :, at] - sign * mine
        v[outer, :, at] = n + change - sign * (flux + theirs)
        v[outermost, :, at] = value + sign * theirs

    def second_part(at):
        full = [v_row(r, at) for r in range(-2, rows + 2)]
        before = None
        for n in range(rows + 1):
            a, b, d, e = full[n : n + 4]
            flux = coef_y[n + 1, :, at] * (7.0 * (b + d) - (a + e))
            if before is not None:
                u[n - 1, :, at] = z[n - 1, :, at] - (flux - before)
            before = flux

    def first_substep(side):
        if side == 0:
            group, outer, faces, other = -2, (0, 1), (-2, -1), ilat - 1
        else:
            group, outer, other = rows // 2, (rows + 2, rows + 3), ilat + 1
            faces = (rows - 1, rows)
        for r in faces:
            set_coef_y(r)
        pieces(functools.partial(halo_part, side))

        @pl.when(jnp.logical_not(there[1 - side]))
        def _():
            for r in outer:
                v[r] = jnp.zeros(v.shape[1:], F32)

        def band_is_polar(band):
            return jnp.logical_or(band < polar, band >= n_lat - polar)

        @pl.when(jnp.logical_or(band_is_polar(ilat), band_is_polar(other)))
        def _():
            low_pass(v, group + 2, group)

        for r in range(max(group, 0), min(group + rows, rows)):
            z[r] = zonal(v_row(r), coef_x[r])

    def low_pass(ref, base, first):
        x = jnp.concatenate([ref[base + j] for j in range(rows)], axis=0)
        cuts = [cut[jnp.clip(ilat * rows + first + j, 0, n_lat * rows - 1)] for j in range(rows)]
        count = x.shape[0]
        stacked = jnp.concatenate([x[:, q * SEG : (q + 1) * SEG] for q in range(segments)], axis=0)
        part = dot3(stacked, fwd_v[0], fwd_v[1])
        real = jnp.zeros((count, KMAX), F32)
        imag = jnp.zeros((count, KMAX), F32)
        for q in range(segments):
            p = part[q * count : (q + 1) * count, 0:KMAX]
            s = part[q * count : (q + 1) * count, KMAX : 2 * KMAX]
            c_q, s_q = turn_v[2 * q : 2 * q + 1, :], turn_v[2 * q + 1 : 2 * q + 2, :]
            real += c_q * p - s_q * s
            imag += s_q * p + c_q * s
        wave = lax.broadcasted_iota(jnp.int32, (2 * levs, KMAX), 1)
        double = jnp.where(wave == 0, 1.0 / length, 2.0 / length).astype(F32)
        weight = jnp.concatenate(
            [jnp.where(wave <= cuts[j], double, 0.0) for j in range(rows)], axis=0
        )
        real, imag = real * weight, imag * weight
        spread = []
        for q in range(segments):
            c_q, s_q = turn_v[2 * q : 2 * q + 1, :], turn_v[2 * q + 1 : 2 * q + 2, :]
            spread.append(
                jnp.concatenate([real * c_q + imag * s_q, imag * c_q - real * s_q], axis=1)
            )
        back = dot3(jnp.concatenate(spread, axis=0), inv_v[0], inv_v[1])
        for q in range(segments):
            for j in range(rows):
                at = q * count + j * 2 * levs
                piece = slice(q * SEG, (q + 1) * SEG)
                ref[base + j, :, piece] = jnp.where(
                    cuts[j] < length // 2, back[at : at + 2 * levs], ref[base + j, :, piece]
                )

    tiles = rows + rows // 2
    low_lane = lax.broadcasted_iota(jnp.int32, (2 * levs, 128), 1) < 64

    def encode(slot, parts):
        most = jnp.abs(parts[0])
        for part in parts[1:]:
            most = jnp.maximum(most, jnp.abs(part))
        power = jnp.ceil(jnp.log2(jnp.maximum(most, 1e-30)) * STEPS + 0.01)
        to_code = jnp.exp2(power * (-1.0 / STEPS)) * CODE_MAX
        for a, part in enumerate(parts):
            code = jnp.clip((part * to_code + ROUNDER) - ROUNDER, -CODE_MAX, CODE_MAX)
            send[slot, a] = code.astype(jnp.int32).astype(jnp.int16)
        send[slot, tiles] = power.astype(jnp.int32).astype(jnp.int16)

    def pack(e):
        def tile(j, t):
            return u[j, :, pl.ds(pl.multiple_of(e * width + t * 128, 128), 128)]

        first = [tile(j, 0) for j in range(rows)]
        second = [tile(j, 2) for j in range(rows)]
        for j in range(0, rows, 2):
            one, two = tile(j, 1), tile(j + 1, 1)
            first.append(jnp.where(low_lane, one, pltpu.roll(two, 64, 1)))
            second.append(jnp.where(low_lane, pltpu.roll(one, 64, 1), two))
        encode(2 * e, first)
        encode(2 * e + 1, second)

    def target(step):
        half = lax.div(step + 1, 2)
        return lax.rem(y + n_y // 2 + jnp.where(lax.rem(step, 2) == 1, -half, half), n_y)

    def column_copy(step, core):
        other = target(step) * 2 + core
        return pltpu.make_async_remote_copy(
            src_ref=send.at[other], dst_ref=recv.at[ilev],
            send_sem=a2a_send.at[step, core], recv_sem=a2a_recv.at[step, parity],
            device_id={"lev": other}, device_id_type=MESH,
        )

    def column_arrival(step, core):
        return pltpu.make_async_remote_copy(
            src_ref=send.at[0], dst_ref=recv.at[ilev],
            send_sem=a2a_send.at[step, core], recv_sem=a2a_recv.at[step, core],
            device_id={"lev": ilev}, device_id_type=MESH,
        )

    def columns(before):
        @pl.loop(0, n_y - 1)
        def _(step):
            e = target(step)
            before(e)
            pack(e)
            column_copy(step, 0).start()
            column_copy(step, 1).start()

        before(y)
        pack(y)
        column_copy(n_y - 1, 1 - parity).start()
        recv[ilev] = send[ilev]

    halo_start(0, 3)
    for load in loads[3:]:
        load.start()
    for load in loads[:2]:
        load.wait()
    stage[0, 0] = u[rows - 2].astype(BF16)
    stage[1, 0] = u[1].astype(BF16)
    halo_start(3, 4)
    loads[2].wait()
    for r in range(rows):
        set_coef_x(r)
        z[r] = zonal(u[r], coef_x[r])
    for r in range(rows - 1):
        set_coef_y(r)
    pieces(own_part)
    halo_start(4, 5)
    tell(ring_one, lev=level(1, parity))
    tell(ring_one, lev=level(-1, parity))
    for load in loads[3:]:
        load.wait()
    write_maps(n_lev, levs, wv, maps)
    halo_wait(1)
    first_substep(1)
    pl.semaphore_wait(ring_one, 2)
    tell(ring_two, lev=level(2, parity))
    tell(ring_two, lev=level(-2, parity))
    halo_wait(0)
    first_substep(0)
    pl.semaphore_wait(ring_two, 2)
    is_polar = jnp.logical_or(ilat < polar, ilat >= n_lat - polar)

    @pl.when(is_polar)
    def _():
        pieces(second_part)
        low_pass(u, 0, 0)
        columns(lambda e: None)

    @pl.when(jnp.logical_not(is_polar))
    def _():
        columns(lambda e: second_part(pl.ds(pl.multiple_of(e * width, 128), width)))

    for side in (0, 1):

        @pl.when(there[side])
        def _():
            for copy in halo_copies(side):
                copy.wait_send()

    @pl.loop(0, n_y - 1)
    def _(step):
        for core in range(2):
            column_copy(step, core).wait_send()
            column_arrival(step, core).wait_recv()

    column_copy(n_y - 1, 1 - parity).wait_send()
    column_arrival(n_y - 1, 1 - parity).wait_recv()


def write_maps(n_lev, levs, wv, maps):
    count = n_lev * levs
    depth = n_lev * 2 * levs
    source = lax.broadcasted_iota(jnp.int32, (count, depth), 1)
    goal = lax.broadcasted_iota(jnp.int32, (count, depth), 0)
    level = lax.div(source, 2 * levs) * levs + lax.rem(source, levs)
    is_heat = lax.rem(source, 2 * levs) >= levs
    scale = count**-0.5
    deeper = jnp.where(level > goal, scale, jnp.where(level == goal, 0.5 * scale, 0.0))
    w_high, w_low = halves(wv[...])
    one_hot = (level == goal).astype(F32).astype(BF16)
    for half, w in enumerate((w_high, w_low)):
        wide = jnp.dot(w, one_hot, preferred_element_type=F32)
        maps[half, 0:count, :] = jnp.where(is_heat, 0.0, wide).astype(BF16)
        maps[half, count : 2 * count, :] = jnp.where(is_heat, wide, 0.0).astype(BF16)
    maps[0, 2 * count : 3 * count, :] = jnp.where(is_heat, deeper, 0.0).astype(BF16)
    maps[1, 2 * count : 3 * count, :] = jnp.zeros((count, depth), BF16)


def remap(recv, maps, surf, out, geo, out_v, geo_v, out_sem, geo_sem):
    n_lev, tiles, depth_rows = recv.shape[0], recv.shape[1] - 1, recv.shape[2]
    rows = surf.shape[0]
    count = maps.shape[1] // 3
    depth = n_lev * depth_rows
    parity = lax.rem(lax.axis_index("lev"), 2)
    scale = jnp.exp2(recv[:, tiles].astype(jnp.int32).astype(F32) * (1.0 / STEPS))
    scale = (scale * (1.0 / CODE_MAX)).reshape(depth, 128)
    values = [
        recv[:, a].astype(jnp.int32).astype(F32).reshape(depth, 128) * scale for a in range(tiles)
    ]
    x_high, x_low = halves(jnp.concatenate(values, axis=1))
    y = jnp.dot(maps[0], x_high, preferred_element_type=F32)
    y += jnp.dot(maps[0], x_low, preferred_element_type=F32)
    y += jnp.dot(maps[1], x_high, preferred_element_type=F32)
    low_out = lax.broadcasted_iota(jnp.int32, (count, 128), 1) < 64

    def put(j, f, first, second):
        if f < 2:
            out_v[f, j, :, 0:128] = first
            out_v[f, j, :, 128:192] = second[:, 0:64]
            pltpu.make_async_copy(out_v.at[f, j], out.at[f, j], out_sem.at[f, j]).start()
        else:
            geo_v[j, :, 0:128] = first
            geo_v[j, :, 128:192] = second[:, 0:64]
            pltpu.make_async_copy(geo_v.at[j], geo.at[j], geo_sem.at[j]).start()

    @pl.when(parity == 0)
    def _():
        for j in range(rows):
            for f in range(3):
                main = y[f * count : (f + 1) * count, j * 128 : (j + 1) * 128]
                at = (rows + j // 2) * 128
                side = y[f * count : (f + 1) * count, at : at + 128]
                if j % 2 == 1:
                    side = pltpu.roll(side, 64, 1)
                if f == 2:
                    main = main + surf[j : j + 1, 0:128]
                    side = side + surf[j : j + 1, 128:256]
                put(j, f, main, side)

    @pl.when(parity == 1)
    def _():
        for j in range(rows):
            for f in range(3):
                main = y[f * count : (f + 1) * count, j * 128 : (j + 1) * 128]
                at = (rows + j // 2) * 128
                side = y[f * count : (f + 1) * count, at : at + 128]
                if f == 2:
                    main = main + surf[j : j + 1, 256:384]
                    ground = surf[j : j + 1, 128:256]
                    side = side + (pltpu.roll(ground, 64, 1) if j % 2 == 0 else ground)
                if j % 2 == 1:
                    side = pltpu.roll(side, 64, 1)
                main = pltpu.roll(main, 64, 1)
                put(j, f, jnp.where(low_out, side, main), main)

    for j in range(rows):
        for f in range(2):
            pltpu.make_async_copy(out_v.at[f, j], out.at[f, j], out_sem.at[f, j]).wait()
        pltpu.make_async_copy(geo_v.at[j], geo.at[j], geo_sem.at[j]).wait()


def solution(mesh):
    n_lat, n_lev = mesh.shape["lat"], mesh.shape["lev"]

    def shards(fields, courant, cutoffs, surface, weights):
        _, rows, levs, length = fields.shape
        fwd, inv, turn = fourier_tables(length)
        count = weights.shape[0]
        tiles = rows + rows // 2
        hbm_spec = pl.BlockSpec(memory_space=pltpu.HBM)
        vmem_spec = pl.BlockSpec(memory_space=pltpu.VMEM)
        dma = pltpu.SemaphoreType.DMA
        recv, maps, surf = pl.pallas_call(
            functools.partial(transport, n_lat, n_lev, 16 // rows),
            name="transport",
            out_shape=(
                pltpu.VMEM((n_lev, tiles + 1, 2 * levs, 128), jnp.int16),
                pltpu.VMEM((2, 3 * count, 2 * count), BF16),
                pltpu.VMEM((rows, 384), F32),
            ),
            in_specs=[hbm_spec] * 8,
            out_specs=(vmem_spec,) * 3,
            scratch_shapes=[
                pltpu.VMEM(courant.shape, BF16),
                pltpu.SMEM(cutoffs.shape, jnp.int32),
                pltpu.VMEM(weights.shape, F32),
                pltpu.VMEM(fwd.shape, BF16),
                pltpu.VMEM(inv.shape, BF16),
                pltpu.VMEM(turn.shape, F32),
                pltpu.VMEM((rows, 2 * levs, length), F32),
                pltpu.VMEM((rows + 4, 2 * levs, length), F32),
                pltpu.VMEM((rows, 2 * levs, length), F32),
                pltpu.VMEM((rows, 2 * levs, length), F32),
                pltpu.VMEM((rows + 3, 2 * levs, length), F32),
                pltpu.VMEM((2, 2 * levs, length), F32),
                pltpu.VMEM((2, 3, 2 * levs, length), BF16),
                pltpu.VMEM((2, 3, 2 * levs, length), BF16),
                pltpu.VMEM((2, 2, levs, length), BF16),
                pltpu.VMEM((n_lev, tiles + 1, 2 * levs, 128), jnp.int16),
                dma((9,)),
                dma((2, 5)),
                dma((2, 5)),
                dma((n_lev // 2, 2)),
                dma((n_lev // 2, 2)),
                pltpu.SemaphoreType.REGULAR,
                pltpu.SemaphoreType.REGULAR,
            ],
            compiler_params=pltpu.CompilerParams(
                collective_id=0, has_side_effects=True
            ),
        )(fields, courant, cutoffs, surface, weights, fwd, inv, turn)
        columns = length // n_lev
        return pl.pallas_call(
            remap,
            name="remap",
            out_shape=(
                jax.ShapeDtypeStruct((2, rows, count, columns), F32),
                jax.ShapeDtypeStruct((rows, count, columns), F32),
            ),
            in_specs=[vmem_spec] * 3,
            out_specs=(hbm_spec, hbm_spec),
            scratch_shapes=[
                pltpu.VMEM((2, rows, count, columns), F32),
                pltpu.VMEM((rows, count, columns), F32),
                dma((2, rows)),
                dma((rows,)),
            ],
            compiler_params=pltpu.CompilerParams(vmem_limit_bytes=24 << 20),
        )(recv, maps, surf)

    return jax.shard_map(
        shards,
        mesh=mesh,
        in_specs=(
            P(None, "lat", "lev", None),
            P(None, "lat", "lev", None),
            P(),
            P("lat", None),
            P(),
        ),
        out_specs=(P(None, "lat", None, "lev"), P("lat", None, "lev")),
        check_vma=False,
    )
```

```python
import functools

import jax
import jax.numpy as jnp
import numpy as np
from jax import lax
from jax.experimental import pallas as pl
from jax.experimental.pallas import tpu as pltpu
from jax.sharding import PartitionSpec as P

MESH = pl.DeviceIdType.MESH
KMAX = 128
SEG = 256
CODE_MAX = 32767.0
ROUNDER = 1.5 * 2.0**23
F32 = jnp.float32
BF16 = jnp.bfloat16


def split_bf16(table):
    high = table.astype(np.float32).astype(jnp.bfloat16)
    low = (table - high.astype(np.float64)).astype(np.float32).astype(jnp.bfloat16)
    return np.stack([high, low])


def fourier_tables(length):
    waves = np.arange(KMAX)
    phase = (np.arange(SEG)[:, None] * waves[None, :]) % length
    angle = phase * (2.0 * np.pi / length)
    inner = np.concatenate([np.cos(angle), np.sin(angle)], axis=1)
    segments = length // SEG
    outer = (np.arange(segments)[:, None] * waves[None, :]) % segments
    outer = outer * (2.0 * np.pi / segments)
    turn = np.stack([np.cos(outer), np.sin(outer)], axis=1).astype(np.float32)
    return split_bf16(inner), split_bf16(inner.T), turn.reshape(2 * segments, KMAX)


def halves(x):
    high = x.astype(BF16)
    return high, (x - high.astype(F32)).astype(BF16)


def dot3(x, high, low):
    x_high, x_low = halves(x)
    out = jnp.dot(x_high, high, preferred_element_type=F32)
    out += jnp.dot(x_low, high, preferred_element_type=F32)
    return out + jnp.dot(x_high, low, preferred_element_type=F32)


def zonal(u, coef):
    length = u.shape[-1]
    pair = u + pltpu.roll(u, length - 1, 1)
    face = 8.0 * pair - (pltpu.roll(pair, 1, 1) + pltpu.roll(pair, length - 1, 1))
    flux = coef * face
    return u - (flux - pltpu.roll(flux, 1, 1))


def transport(
    n_lat, n_lev, polar,
    fields, courant, cutoffs, surface, weights, fwd, inv, turn,
    x_high, x_low, maps, surf,
    cv, cut, wv, fwd_v, inv_v, turn_v,
    u, v, z, coef_x, coef_y, near, near_sent, near_got, near_scale, far, stage, cy_halo, send, recv, send_scale, recv_scale,
    in_sem, halo_send, halo_recv, a2a_send, a2a_recv, scale_sent, scale_got,
    ring_one, ring_two,
):
    ilat, ilev = lax.axis_index("lat"), lax.axis_index("lev")
    rows, length = u.shape[0], u.shape[2]
    levs = u.shape[1] // 2
    segments = length // SEG
    n_y = n_lev // 2
    y, parity = lax.div(ilev, 2), lax.rem(ilev, 2)
    width = 3 * 128

    loads = [
        pltpu.make_async_copy(fields.at[0], u.at[:, 0:levs, :], in_sem.at[0]),
        pltpu.make_async_copy(fields.at[1], u.at[:, levs : 2 * levs, :], in_sem.at[1]),
        pltpu.make_async_copy(courant, cv, in_sem.at[2]),
        pltpu.make_async_copy(weights, wv, in_sem.at[5]),
        pltpu.make_async_copy(cutoffs, cut, in_sem.at[3]),
        pltpu.make_async_copy(
            surface.at[:, pl.ds(pl.multiple_of(y * width, 128), width)], surf, in_sem.at[4]
        ),
        pltpu.make_async_copy(fwd, fwd_v, in_sem.at[6]),
        pltpu.make_async_copy(inv, inv_v, in_sem.at[7]),
        pltpu.make_async_copy(turn, turn_v, in_sem.at[8]),
    ]

    has_minus, has_plus = ilat > 0, ilat < n_lat - 1
    barrier = pltpu.get_barrier_semaphore()

    def tell(sem, **where):
        pl.semaphore_signal(sem, inc=1, device_id=where, device_id_type=MESH)

    def level(step, core):
        return lax.rem(y + step + n_y, n_y) * 2 + core

    @pl.when(has_minus)
    def _():
        tell(barrier, lat=ilat - 1)

    @pl.when(has_plus)
    def _():
        tell(barrier, lat=ilat + 1)

    for core in range(2):
        tell(barrier, lev=level(1, core))
        tell(barrier, lev=level(-1, core))
    tell(barrier, lev=level(0, 1 - parity))

    for load in loads[:3]:
        load.start()

    neighbours = has_minus.astype(jnp.int32) + has_plus.astype(jnp.int32)
    pl.semaphore_wait(barrier, 5 + neighbours)

    def halo_copies(side):
        pieces = [
            (courant.at[1, pl.ds((rows - 2, 0)[side], 2)], cy_halo.at[side]),
            (near_scale.at[0, side], near_scale.at[1, side]),
            (near_sent.at[side], near_got.at[side]),
            (stage.at[side, 0], far.at[side, 0]),
            (stage.at[side, pl.ds(1, 2)], far.at[side, pl.ds(1, 2)]),
        ]
        return [
            pltpu.make_async_remote_copy(
                src_ref=source, dst_ref=goal,
                send_sem=halo_send.at[side, n], recv_sem=halo_recv.at[side, n],
                device_id={"lat": ilat + (1, -1)[side]}, device_id_type=MESH,
            )
            for n, (source, goal) in enumerate(pieces)
        ]

    there = (has_plus, has_minus)

    def halo_start(first, last):
        for side in (0, 1):

            @pl.when(there[side])
            def _():
                for copy in halo_copies(side)[first:last]:
                    copy.start()

    def halo_wait(side):
        @pl.when(there[1 - side])
        def _():
            for copy in halo_copies(side):
                copy.wait_recv()

        @pl.when(jnp.logical_not(there[1 - side]))
        def _():
            near_got[side] = jnp.zeros(near_got.shape[1:], jnp.int16)
            near_scale[1, side] = jnp.zeros(near_scale.shape[2:], F32)
            far[side] = jnp.zeros(far.shape[1:], BF16)
            cy_halo[side] = jnp.zeros(cy_halo.shape[1:], BF16)

    def both(x):
        return jnp.concatenate([x, x], axis=0)

    def cy_row(r):
        if r < 0:
            return both(cy_halo[0, r + 2].astype(F32))
        if r >= rows:
            return both(cy_halo[1, r - rows].astype(F32))
        return both(cv[1, r].astype(F32))

    def spans():
        return [slice(t * 128, (t + 1) * 128) for t in range(length // 128)]

    def send_near(side):
        row = (rows - 1, 0)[side]
        most = jnp.full((2 * levs, 128), 1e-30, F32)
        for at in spans():
            most = jnp.maximum(most, jnp.abs(u[row, :, at]))
        most = jnp.max(most, axis=0, keepdims=True)
        near_scale[0, side] = most * (1.0 / CODE_MAX)
        to_code = CODE_MAX / most
        for at in spans():
            code = (u[row, :, at] * to_code + ROUNDER) - ROUNDER
            near_sent[side, :, at] = code.astype(jnp.int32).astype(jnp.int16)

    def take_near(side):
        for at in spans():
            near[side, :, at] = near_got[side, :, at].astype(jnp.int32).astype(F32) * near_scale[1, side]

    def v_row(r, at=slice(None)):
        return v[r + 2, :, at]

    def set_coef_x(r):
        cx = both(cv[0, r].astype(F32))
        coef_x[r] = (cx + pltpu.roll(cx, length - 1, 1)) * (1.0 / 24.0)

    def set_coef_y(r):
        coef_y[r + 2] = (cy_row(r) + cy_row(r + 1)) * (1.0 / 24.0)

    def pieces(body, piece=512):
        @pl.loop(0, length // piece)
        def _(c):
            body(pl.ds(pl.multiple_of(c * piece, 128), piece))

    def own_part(at):
        u0, u1, u2, u3 = (u[r, :, at] for r in range(4))
        low = coef_y[2, :, at] * (7.0 * (u0 + u1) - u2)
        middle = coef_y[3, :, at] * (7.0 * (u1 + u2) - (u0 + u3))
        high = coef_y[4, :, at] * (7.0 * (u2 + u3) - u1)
        z0, z1 = z[0, :, at] - low, z[1, :, at] - middle + low
        z2, z3 = z[2, :, at] - high + middle, z[3, :, at] + high
        z[0, :, at], z[1, :, at], z[2, :, at], z[3, :, at] = z0, z1, z2, z3
        stage[0, 1, :, at] = (z3 - u3).astype(BF16)
        stage[0, 2, :, at] = z2.astype(BF16)
        stage[1, 1, :, at] = (z0 - u0).astype(BF16)
        stage[1, 2, :, at] = z1.astype(BF16)

    def halo_part(side, at):
        edge, inner, sign = ((0, 1, 1.0), (rows - 1, rows - 2, -1.0))[side]
        outer, outermost = ((1, 0), (rows + 2, rows + 3))[side]
        beyond, shared, inside = ((0, 1, 2), (rows + 2, rows + 1, rows))[side]
        n, f = near[side, :, at], far[side, 0, :, at].astype(F32)
        change, value = far[side, 1, :, at].astype(F32), far[side, 2, :, at].astype(F32)
        flux = coef_y[shared, :, at] * (7.0 * (n + u[edge, :, at]) - (f + u[inner, :, at]))
        mine = coef_y[inside, :, at] * n
        theirs = coef_y[beyond, :, at] * u[edge, :, at]
        v[edge + 2, :, at] = z[edge, :, at] + sign * (mine + flux)
        v[inner + 2, :, at] = z[inner, :, at] - sign * mine
        v[outer, :, at] = n + change - sign * (flux + theirs)
        v[outermost, :, at] = value + sign * theirs

    def second_part(at):
        full = [v_row(r, at) for r in range(-2, rows + 2)]
        before = None
        for n in range(rows + 1):
            a, b, d, e = full[n : n + 4]
            flux = coef_y[n + 1, :, at] * (7.0 * (b + d) - (a + e))
            if before is not None:
                u[n - 1, :, at] = z[n - 1, :, at] - (flux - before)
            before = flux

    def first_substep(side):
        if side == 0:
            group, outer, faces, other = -2, (0, 1), (-2, -1), ilat - 1
        else:
            group, outer, other = rows // 2, (rows + 2, rows + 3), ilat + 1
            faces = (rows - 1, rows)
        take_near(side)
        for r in faces:
            set_coef_y(r)
        pieces(functools.partial(halo_part, side))

        @pl.when(jnp.logical_not(there[1 - side]))
        def _():
            for r in outer:
                v[r] = jnp.zeros(v.shape[1:], F32)

        def band_is_polar(band):
            return jnp.logical_or(band < polar, band >= n_lat - polar)

        @pl.when(jnp.logical_or(band_is_polar(ilat), band_is_polar(other)))
        def _():
            low_pass(v, group + 2, group)

        for r in range(max(group, 0), min(group + rows, rows)):
            z[r] = zonal(v_row(r), coef_x[r])

    def low_pass(ref, base, first):
        x = jnp.concatenate([ref[base + j] for j in range(rows)], axis=0)
        cuts = [cut[jnp.clip(ilat * rows + first + j, 0, n_lat * rows - 1)] for j in range(rows)]
        count = x.shape[0]
        stacked = jnp.concatenate([x[:, q * SEG : (q + 1) * SEG] for q in range(segments)], axis=0)
        part = dot3(stacked, fwd_v[0], fwd_v[1])
        real = jnp.zeros((count, KMAX), F32)
        imag = jnp.zeros((count, KMAX), F32)
        for q in range(segments):
            p = part[q * count : (q + 1) * count, 0:KMAX]
            s = part[q * count : (q + 1) * count, KMAX : 2 * KMAX]
            c_q, s_q = turn_v[2 * q : 2 * q + 1, :], turn_v[2 * q + 1 : 2 * q + 2, :]
            real += c_q * p - s_q * s
            imag += s_q * p + c_q * s
        wave = lax.broadcasted_iota(jnp.int32, (2 * levs, KMAX), 1)
        double = jnp.where(wave == 0, 1.0 / length, 2.0 / length).astype(F32)
        weight = jnp.concatenate(
            [jnp.where(wave <= cuts[j], double, 0.0) for j in range(rows)], axis=0
        )
        real, imag = real * weight, imag * weight
        spread = []
        for q in range(segments):
            c_q, s_q = turn_v[2 * q : 2 * q + 1, :], turn_v[2 * q + 1 : 2 * q + 2, :]
            spread.append(
                jnp.concatenate([real * c_q + imag * s_q, imag * c_q - real * s_q], axis=1)
            )
        back = dot3(jnp.concatenate(spread, axis=0), inv_v[0], inv_v[1])
        for q in range(segments):
            for j in range(rows):
                at = q * count + j * 2 * levs
                piece = slice(q * SEG, (q + 1) * SEG)
                ref[base + j, :, piece] = jnp.where(
                    cuts[j] < length // 2, back[at : at + 2 * levs], ref[base + j, :, piece]
                )

    tiles = rows + rows // 2
    low_lane = lax.broadcasted_iota(jnp.int32, (2 * levs, 128), 1) < 64

    def encode(slot, parts):
        most = jnp.abs(parts[0])
        for part in parts[1:]:
            most = jnp.maximum(most, jnp.abs(part))
        most = jnp.maximum(jnp.max(most, axis=0, keepdims=True), 1e-30)
        to_code = CODE_MAX / most
        send_scale[slot] = most * (1.0 / CODE_MAX)
        for a, part in enumerate(parts):
            code = (part * to_code + ROUNDER) - ROUNDER
            send[slot, a] = code.astype(jnp.int32).astype(jnp.int16)

    def pack(e):
        def tile(j, t):
            return u[j, :, pl.ds(pl.multiple_of(e * width + t * 128, 128), 128)]

        first = [tile(j, 0) for j in range(rows)]
        second = [tile(j, 2) for j in range(rows)]
        for j in range(0, rows, 2):
            one, two = tile(j, 1), tile(j + 1, 1)
            first.append(jnp.where(low_lane, one, pltpu.roll(two, 64, 1)))
            second.append(jnp.where(low_lane, pltpu.roll(one, 64, 1), two))
        encode(2 * e, first)
        encode(2 * e + 1, second)

    def target(step):
        half = lax.div(step + 1, 2)
        return lax.rem(y + n_y // 2 + jnp.where(lax.rem(step, 2) == 1, -half, half), n_y)

    def column_copies(step, core):
        other = target(step) * 2 + core
        return [
            pltpu.make_async_remote_copy(
                src_ref=source.at[other], dst_ref=goal.at[ilev],
                send_sem=sent.at[step, core], recv_sem=got.at[step, parity],
                device_id={"lev": other}, device_id_type=MESH,
            )
            for source, goal, sent, got in (
                (send_scale, recv_scale, scale_sent, scale_got),
                (send, recv, a2a_send, a2a_recv),
            )
        ]

    def column_start(step, core):
        for copy in column_copies(step, core):
            copy.start()

    def column_wait(step, core):
        for source, goal, sent, got in (
            (send_scale, recv_scale, scale_sent, scale_got),
            (send, recv, a2a_send, a2a_recv),
        ):
            pltpu.make_async_remote_copy(
                src_ref=source.at[0], dst_ref=goal.at[ilev],
                send_sem=sent.at[step, core], recv_sem=got.at[step, core],
                device_id={"lev": ilev}, device_id_type=MESH,
            ).wait_recv()

    def decode(chip):
        for a in range(tiles):
            parts = []
            for core in range(2):
                code = recv[2 * chip + core, a].astype(jnp.int32).astype(F32)
                parts.append(code * recv_scale[2 * chip + core])
            high, low = halves(jnp.concatenate(parts, axis=0))
            at = pl.ds(pl.multiple_of(chip * 4 * levs, 4 * levs), 4 * levs)
            x_high[at, a * 128 : (a + 1) * 128] = high
            x_low[at, a * 128 : (a + 1) * 128] = low

    def columns(before):
        @pl.loop(0, n_y - 1)
        def _(step):
            e = target(step)
            before(e)
            pack(e)
            column_start(step, 0)
            column_start(step, 1)

        before(y)
        pack(y)
        column_start(n_y - 1, 1 - parity)
        recv[ilev] = send[ilev]
        recv_scale[ilev] = send_scale[ilev]

    halo_start(0, 1)
    for load in loads[3:]:
        load.start()
    for load in loads[:2]:
        load.wait()
    send_near(0)
    send_near(1)
    halo_start(1, 3)
    stage[0, 0] = u[rows - 2].astype(BF16)
    stage[1, 0] = u[1].astype(BF16)
    halo_start(3, 4)
    loads[2].wait()
    for r in range(rows):
        set_coef_x(r)
        z[r] = zonal(u[r], coef_x[r])
    for r in range(rows - 1):
        set_coef_y(r)
    pieces(own_part)
    halo_start(4, 5)
    tell(ring_one, lev=level(1, parity))
    tell(ring_one, lev=level(-1, parity))
    for load in loads[3:]:
        load.wait()
    write_maps(n_lev, levs, wv, maps)
    halo_wait(1)
    first_substep(1)
    pl.semaphore_wait(ring_one, 2)
    tell(ring_two, lev=level(2, parity))
    tell(ring_two, lev=level(-2, parity))
    halo_wait(0)
    first_substep(0)
    pl.semaphore_wait(ring_two, 2)
    is_polar = jnp.logical_or(ilat < polar, ilat >= n_lat - polar)

    @pl.when(is_polar)
    def _():
        pieces(second_part)
        low_pass(u, 0, 0)
        columns(lambda e: None)

    @pl.when(jnp.logical_not(is_polar))
    def _():
        columns(lambda e: second_part(pl.ds(pl.multiple_of(e * width, 128), width)))

    for side in (0, 1):

        @pl.when(there[side])
        def _():
            for copy in halo_copies(side):
                copy.wait_send()

    column_wait(n_y - 1, 1 - parity)
    decode(y)

    @pl.loop(1, n_y)
    def _(lap):
        step = n_y - 1 - lap
        column_wait(step, 0)
        column_wait(step, 1)
        decode(lax.rem(2 * y + n_y - target(step), n_y))

    @pl.loop(0, n_y - 1)
    def _(step):
        for core in range(2):
            for copy in column_copies(step, core):
                copy.wait_send()

    for copy in column_copies(n_y - 1, 1 - parity):
        copy.wait_send()


def write_maps(n_lev, levs, wv, maps):
    count = n_lev * levs
    depth = n_lev * 2 * levs
    source = lax.broadcasted_iota(jnp.int32, (count, depth), 1)
    goal = lax.broadcasted_iota(jnp.int32, (count, depth), 0)
    level = lax.div(source, 2 * levs) * levs + lax.rem(source, levs)
    is_heat = lax.rem(source, 2 * levs) >= levs
    scale = count**-0.5
    deeper = jnp.where(level > goal, scale, jnp.where(level == goal, 0.5 * scale, 0.0))
    w_high, w_low = halves(wv[...])
    one_hot = (level == goal).astype(F32).astype(BF16)
    for half, w in enumerate((w_high, w_low)):
        wide = jnp.dot(w, one_hot, preferred_element_type=F32)
        maps[half, 0:count, :] = jnp.where(is_heat, 0.0, wide).astype(BF16)
        maps[half, count : 2 * count, :] = jnp.where(is_heat, wide, 0.0).astype(BF16)
    maps[0, 2 * count : 3 * count, :] = jnp.where(is_heat, deeper, 0.0).astype(BF16)
    maps[1, 2 * count : 3 * count, :] = jnp.zeros((count, depth), BF16)


def remap(x_high, x_low, maps, surf, out, geo, out_v, geo_v, out_sem, geo_sem):
    rows = surf.shape[0]
    count = maps.shape[1] // 3
    parity = lax.rem(lax.axis_index("lev"), 2)
    y = jnp.dot(maps[0], x_high[...], preferred_element_type=F32)
    y += jnp.dot(maps[0], x_low[...], preferred_element_type=F32)
    y += jnp.dot(maps[1], x_high[...], preferred_element_type=F32)
    low_out = lax.broadcasted_iota(jnp.int32, (count, 128), 1) < 64

    def put(j, f, first, second):
        if f < 2:
            out_v[f, j, :, 0:128] = first
            out_v[f, j, :, 128:192] = second[:, 0:64]
            pltpu.make_async_copy(out_v.at[f, j], out.at[f, j], out_sem.at[f, j]).start()
        else:
            geo_v[j, :, 0:128] = first
            geo_v[j, :, 128:192] = second[:, 0:64]
            pltpu.make_async_copy(geo_v.at[j], geo.at[j], geo_sem.at[j]).start()

    @pl.when(parity == 0)
    def _():
        for j in range(rows):
            for f in range(3):
                main = y[f * count : (f + 1) * count, j * 128 : (j + 1) * 128]
                at = (rows + j // 2) * 128
                side = y[f * count : (f + 1) * count, at : at + 128]
                if j % 2 == 1:
                    side = pltpu.roll(side, 64, 1)
                if f == 2:
                    main = main + surf[j : j + 1, 0:128]
                    side = side + surf[j : j + 1, 128:256]
                put(j, f, main, side)

    @pl.when(parity == 1)
    def _():
        for j in range(rows):
            for f in range(3):
                main = y[f * count : (f + 1) * count, j * 128 : (j + 1) * 128]
                at = (rows + j // 2) * 128
                side = y[f * count : (f + 1) * count, at : at + 128]
                if f == 2:
                    main = main + surf[j : j + 1, 256:384]
                    ground = surf[j : j + 1, 128:256]
                    side = side + (pltpu.roll(ground, 64, 1) if j % 2 == 0 else ground)
                if j % 2 == 1:
                    side = pltpu.roll(side, 64, 1)
                main = pltpu.roll(main, 64, 1)
                put(j, f, jnp.where(low_out, side, main), main)

    for j in range(rows):
        for f in range(2):
            pltpu.make_async_copy(out_v.at[f, j], out.at[f, j], out_sem.at[f, j]).wait()
        pltpu.make_async_copy(geo_v.at[j], geo.at[j], geo_sem.at[j]).wait()


def solution(mesh):
    n_lat, n_lev = mesh.shape["lat"], mesh.shape["lev"]

    def shards(fields, courant, cutoffs, surface, weights):
        _, rows, levs, length = fields.shape
        fwd, inv, turn = fourier_tables(length)
        count = weights.shape[0]
        tiles = rows + rows // 2
        hbm_spec = pl.BlockSpec(memory_space=pltpu.HBM)
        vmem_spec = pl.BlockSpec(memory_space=pltpu.VMEM)
        dma = pltpu.SemaphoreType.DMA
        parts = pl.pallas_call(
            functools.partial(transport, n_lat, n_lev, 16 // rows),
            name="transport",
            out_shape=(
                pltpu.VMEM((2 * count, tiles * 128), BF16),
                pltpu.VMEM((2 * count, tiles * 128), BF16),
                pltpu.VMEM((2, 3 * count, 2 * count), BF16),
                pltpu.VMEM((rows, 384), F32),
            ),
            in_specs=[hbm_spec] * 8,
            out_specs=(vmem_spec,) * 4,
            scratch_shapes=[
                pltpu.VMEM(courant.shape, BF16),
                pltpu.SMEM(cutoffs.shape, jnp.int32),
                pltpu.VMEM(weights.shape, F32),
                pltpu.VMEM(fwd.shape, BF16),
                pltpu.VMEM(inv.shape, BF16),
                pltpu.VMEM(turn.shape, F32),
                pltpu.VMEM((rows, 2 * levs, length), F32),
                pltpu.VMEM((rows + 4, 2 * levs, length), F32),
                pltpu.VMEM((rows, 2 * levs, length), F32),
                pltpu.VMEM((rows, 2 * levs, length), F32),
                pltpu.VMEM((rows + 3, 2 * levs, length), F32),
                pltpu.VMEM((2, 2 * levs, length), F32),
                pltpu.VMEM((2, 2 * levs, length), jnp.int16),
                pltpu.VMEM((2, 2 * levs, length), jnp.int16),
                pltpu.VMEM((2, 2, 1, 128), F32),
                pltpu.VMEM((2, 3, 2 * levs, length), BF16),
                pltpu.VMEM((2, 3, 2 * levs, length), BF16),
                pltpu.VMEM((2, 2, levs, length), BF16),
                pltpu.VMEM((n_lev, tiles, 2 * levs, 128), jnp.int16),
                pltpu.VMEM((n_lev, tiles, 2 * levs, 128), jnp.int16),
                pltpu.VMEM((n_lev, 1, 128), F32),
                pltpu.VMEM((n_lev, 1, 128), F32),
                dma((9,)),
                dma((2, 5)),
                dma((2, 5)),
                dma((n_lev // 2, 2)),
                dma((n_lev // 2, 2)),
                dma((n_lev // 2, 2)),
                dma((n_lev // 2, 2)),
                pltpu.SemaphoreType.REGULAR,
                pltpu.SemaphoreType.REGULAR,
            ],
            compiler_params=pltpu.CompilerParams(
                collective_id=0, has_side_effects=True
            ),
        )(fields, courant, cutoffs, surface, weights, fwd, inv, turn)
        columns = length // n_lev
        return pl.pallas_call(
            remap,
            name="remap",
            out_shape=(
                jax.ShapeDtypeStruct((2, rows, count, columns), F32),
                jax.ShapeDtypeStruct((rows, count, columns), F32),
            ),
            in_specs=[vmem_spec] * 4,
            out_specs=(hbm_spec, hbm_spec),
            scratch_shapes=[
                pltpu.VMEM((2, rows, count, columns), F32),
                pltpu.VMEM((rows, count, columns), F32),
                dma((2, rows)),
                dma((rows,)),
            ],
            compiler_params=pltpu.CompilerParams(vmem_limit_bytes=24 << 20),
        )(*parts)

    return jax.shard_map(
        shards,
        mesh=mesh,
        in_specs=(
            P(None, "lat", "lev", None),
            P(None, "lat", "lev", None),
            P(),
            P("lat", None),
            P(),
        ),
        out_specs=(P(None, "lat", None, "lev"), P("lat", None, "lev")),
        check_vma=False,
    )
```

```python
import functools

import jax
import jax.numpy as jnp
import numpy as np
from jax import lax
from jax.experimental import pallas as pl
from jax.experimental.pallas import tpu as pltpu
from jax.sharding import PartitionSpec as P

MESH = pl.DeviceIdType.MESH
KMAX = 128
SEG = 256
CODE_MAX = 32767.0
ROUNDER = 1.5 * 2.0**23
F32 = jnp.float32
BF16 = jnp.bfloat16


def split_bf16(table):
    high = table.astype(np.float32).astype(jnp.bfloat16)
    low = (table - high.astype(np.float64)).astype(np.float32).astype(jnp.bfloat16)
    return np.stack([high, low])


def fourier_tables(length):
    waves = np.arange(KMAX)
    phase = (np.arange(SEG)[:, None] * waves[None, :]) % length
    angle = phase * (2.0 * np.pi / length)
    inner = np.concatenate([np.cos(angle), np.sin(angle)], axis=1)
    segments = length // SEG
    outer = (np.arange(segments)[:, None] * waves[None, :]) % segments
    outer = outer * (2.0 * np.pi / segments)
    turn = np.stack([np.cos(outer), np.sin(outer)], axis=1).astype(np.float32)
    return split_bf16(inner), split_bf16(inner.T), turn.reshape(2 * segments, KMAX)


def halves(x):
    high = x.astype(BF16)
    return high, (x - high.astype(F32)).astype(BF16)


def dot3(x, high, low):
    x_high, x_low = halves(x)
    out = jnp.dot(x_high, high, preferred_element_type=F32)
    out += jnp.dot(x_low, high, preferred_element_type=F32)
    return out + jnp.dot(x_high, low, preferred_element_type=F32)


def zonal(u, coef):
    length = u.shape[-1]
    pair = u + pltpu.roll(u, length - 1, 1)
    face = 8.0 * pair - (pltpu.roll(pair, 1, 1) + pltpu.roll(pair, length - 1, 1))
    flux = coef * face
    return u - (flux - pltpu.roll(flux, 1, 1))


def transport(
    n_lat, n_lev, polar,
    fields, courant, cutoffs, surface, weights, fwd, inv, turn,
    x_high, x_low, maps, surf,
    cv, cut, wv, fwd_v, inv_v, turn_v,
    u, v, z, coef_x, coef_y, near, near_sent, near_got, near_scale, far, stage, cy_halo, send, recv, send_scale, recv_scale,
    in_sem, halo_send, halo_recv, a2a_send, a2a_recv, scale_sent, scale_got,
    ring_one, ring_two,
):
    ilat, ilev = lax.axis_index("lat"), lax.axis_index("lev")
    rows, length = u.shape[0], u.shape[2]
    levs = u.shape[1] // 2
    segments = length // SEG
    n_y = n_lev // 2
    y, parity = lax.div(ilev, 2), lax.rem(ilev, 2)
    width = 3 * 128

    loads = [
        pltpu.make_async_copy(fields.at[0], u.at[:, 0:levs, :], in_sem.at[0]),
        pltpu.make_async_copy(fields.at[1], u.at[:, levs : 2 * levs, :], in_sem.at[1]),
        pltpu.make_async_copy(courant, cv, in_sem.at[2]),
        pltpu.make_async_copy(weights, wv, in_sem.at[5]),
        pltpu.make_async_copy(cutoffs, cut, in_sem.at[3]),
        pltpu.make_async_copy(
            surface.at[:, pl.ds(pl.multiple_of(y * width, 128), width)], surf, in_sem.at[4]
        ),
        pltpu.make_async_copy(fwd, fwd_v, in_sem.at[6]),
        pltpu.make_async_copy(inv, inv_v, in_sem.at[7]),
        pltpu.make_async_copy(turn, turn_v, in_sem.at[8]),
    ]

    has_minus, has_plus = ilat > 0, ilat < n_lat - 1
    barrier = pltpu.get_barrier_semaphore()

    def tell(sem, **where):
        pl.semaphore_signal(sem, inc=1, device_id=where, device_id_type=MESH)

    def level(step, core):
        return lax.rem(y + step + n_y, n_y) * 2 + core

    @pl.when(has_minus)
    def _():
        tell(barrier, lat=ilat - 1)

    @pl.when(has_plus)
    def _():
        tell(barrier, lat=ilat + 1)

    for core in range(2):
        tell(barrier, lev=level(1, core))
        tell(barrier, lev=level(-1, core))
    tell(barrier, lev=level(0, 1 - parity))

    for load in loads[:3]:
        load.start()

    neighbours = has_minus.astype(jnp.int32) + has_plus.astype(jnp.int32)
    pl.semaphore_wait(barrier, 5 + neighbours)

    def halo_copies(side):
        pieces = [
            (cv.at[1, pl.ds((rows - 2, 0)[side], 2)], cy_halo.at[side]),
            (near_scale.at[0, side], near_scale.at[1, side]),
            (near_sent.at[side], near_got.at[side]),
            (stage.at[side, 0], far.at[side, 0]),
            (stage.at[side, pl.ds(1, 2)], far.at[side, pl.ds(1, 2)]),
        ]
        return [
            pltpu.make_async_remote_copy(
                src_ref=source, dst_ref=goal,
                send_sem=halo_send.at[side, n], recv_sem=halo_recv.at[side, n],
                device_id={"lat": ilat + (1, -1)[side]}, device_id_type=MESH,
            )
            for n, (source, goal) in enumerate(pieces)
        ]

    there = (has_plus, has_minus)

    def halo_start(first, last):
        for side in (0, 1):

            @pl.when(there[side])
            def _():
                for copy in halo_copies(side)[first:last]:
                    copy.start()

    def halo_wait(side):
        @pl.when(there[1 - side])
        def _():
            for copy in halo_copies(side):
                copy.wait_recv()

        @pl.when(jnp.logical_not(there[1 - side]))
        def _():
            near_got[side] = jnp.zeros(near_got.shape[1:], jnp.int16)
            near_scale[1, side] = jnp.zeros(near_scale.shape[2:], F32)
            far[side] = jnp.zeros(far.shape[1:], BF16)
            cy_halo[side] = jnp.zeros(cy_halo.shape[1:], BF16)

    def both(x):
        return jnp.concatenate([x, x], axis=0)

    def cy_row(r):
        if r < 0:
            return both(cy_halo[0, r + 2].astype(F32))
        if r >= rows:
            return both(cy_halo[1, r - rows].astype(F32))
        return both(cv[1, r].astype(F32))

    def spans():
        return [slice(t * 128, (t + 1) * 128) for t in range(length // 128)]

    def send_near(side):
        row = (rows - 1, 0)[side]
        most = jnp.full((2 * levs, 128), 1e-30, F32)
        for at in spans():
            most = jnp.maximum(most, jnp.abs(u[row, :, at]))
        most = jnp.max(most, axis=0, keepdims=True)
        near_scale[0, side] = most * (1.0 / CODE_MAX)
        to_code = CODE_MAX / most
        for at in spans():
            code = (u[row, :, at] * to_code + ROUNDER) - ROUNDER
            near_sent[side, :, at] = code.astype(jnp.int32).astype(jnp.int16)

    def take_near(side):
        for at in spans():
            near[side, :, at] = near_got[side, :, at].astype(jnp.int32).astype(F32) * near_scale[1, side]

    def v_row(r, at=slice(None)):
        return v[r + 2, :, at]

    def set_coef_x(r):
        cx = both(cv[0, r].astype(F32))
        coef_x[r] = (cx + pltpu.roll(cx, length - 1, 1)) * (1.0 / 24.0)

    def set_coef_y(r):
        coef_y[r + 2] = (cy_row(r) + cy_row(r + 1)) * (1.0 / 24.0)

    def pieces(body, piece=512):
        @pl.loop(0, length // piece)
        def _(c):
            body(pl.ds(pl.multiple_of(c * piece, 128), piece))

    def own_part(at):
        u0, u1, u2, u3 = (u[r, :, at] for r in range(4))
        low = coef_y[2, :, at] * (7.0 * (u0 + u1) - u2)
        middle = coef_y[3, :, at] * (7.0 * (u1 + u2) - (u0 + u3))
        high = coef_y[4, :, at] * (7.0 * (u2 + u3) - u1)
        z0, z1 = z[0, :, at] - low, z[1, :, at] - middle + low
        z2, z3 = z[2, :, at] - high + middle, z[3, :, at] + high
        z[0, :, at], z[1, :, at], z[2, :, at], z[3, :, at] = z0, z1, z2, z3
        stage[0, 1, :, at] = (z3 - u3).astype(BF16)
        stage[0, 2, :, at] = z2.astype(BF16)
        stage[1, 1, :, at] = (z0 - u0).astype(BF16)
        stage[1, 2, :, at] = z1.astype(BF16)

    def halo_part(side, at):
        edge, inner, sign = ((0, 1, 1.0), (rows - 1, rows - 2, -1.0))[side]
        outer, outermost = ((1, 0), (rows + 2, rows + 3))[side]
        beyond, shared, inside = ((0, 1, 2), (rows + 2, rows + 1, rows))[side]
        n, f = near[side, :, at], far[side, 0, :, at].astype(F32)
        change, value = far[side, 1, :, at].astype(F32), far[side, 2, :, at].astype(F32)
        flux = coef_y[shared, :, at] * (7.0 * (n + u[edge, :, at]) - (f + u[inner, :, at]))
        mine = coef_y[inside, :, at] * n
        theirs = coef_y[beyond, :, at] * u[edge, :, at]
        v[edge + 2, :, at] = z[edge, :, at] + sign * (mine + flux)
        v[inner + 2, :, at] = z[inner, :, at] - sign * mine
        v[outer, :, at] = n + change - sign * (flux + theirs)
        v[outermost, :, at] = value + sign * theirs

    def second_part(at):
        full = [v_row(r, at) for r in range(-2, rows + 2)]
        before = None
        for n in range(rows + 1):
            a, b, d, e = full[n : n + 4]
            flux = coef_y[n + 1, :, at] * (7.0 * (b + d) - (a + e))
            if before is not None:
                u[n - 1, :, at] = z[n - 1, :, at] - (flux - before)
            before = flux

    def first_substep(side):
        if side == 0:
            group, outer, faces, other = -2, (0, 1), (-2, -1), ilat - 1
        else:
            group, outer, other = rows // 2, (rows + 2, rows + 3), ilat + 1
            faces = (rows - 1, rows)
        take_near(side)
        for r in faces:
            set_coef_y(r)
        pieces(functools.partial(halo_part, side))

        @pl.when(jnp.logical_not(there[1 - side]))
        def _():
            for r in outer:
                v[r] = jnp.zeros(v.shape[1:], F32)

        def band_is_polar(band):
            return jnp.logical_or(band < polar, band >= n_lat - polar)

        @pl.when(jnp.logical_or(band_is_polar(ilat), band_is_polar(other)))
        def _():
            low_pass(v, group + 2, group)

        for r in range(max(group, 0), min(group + rows, rows)):
            z[r] = zonal(v_row(r), coef_x[r])

    def low_pass(ref, base, first):
        x = jnp.concatenate([ref[base + j] for j in range(rows)], axis=0)
        cuts = [cut[jnp.clip(ilat * rows + first + j, 0, n_lat * rows - 1)] for j in range(rows)]
        count = x.shape[0]
        stacked = jnp.concatenate([x[:, q * SEG : (q + 1) * SEG] for q in range(segments)], axis=0)
        part = dot3(stacked, fwd_v[0], fwd_v[1])
        real = jnp.zeros((count, KMAX), F32)
        imag = jnp.zeros((count, KMAX), F32)
        for q in range(segments):
            p = part[q * count : (q + 1) * count, 0:KMAX]
            s = part[q * count : (q + 1) * count, KMAX : 2 * KMAX]
            c_q, s_q = turn_v[2 * q : 2 * q + 1, :], turn_v[2 * q + 1 : 2 * q + 2, :]
            real += c_q * p - s_q * s
            imag += s_q * p + c_q * s
        wave = lax.broadcasted_iota(jnp.int32, (2 * levs, KMAX), 1)
        double = jnp.where(wave == 0, 1.0 / length, 2.0 / length).astype(F32)
        weight = jnp.concatenate(
            [jnp.where(wave <= cuts[j], double, 0.0) for j in range(rows)], axis=0
        )
        real, imag = real * weight, imag * weight
        spread = []
        for q in range(segments):
            c_q, s_q = turn_v[2 * q : 2 * q + 1, :], turn_v[2 * q + 1 : 2 * q + 2, :]
            spread.append(
                jnp.concatenate([real * c_q + imag * s_q, imag * c_q - real * s_q], axis=1)
            )
        back = dot3(jnp.concatenate(spread, axis=0), inv_v[0], inv_v[1])
        for q in range(segments):
            for j in range(rows):
                at = q * count + j * 2 * levs
                piece = slice(q * SEG, (q + 1) * SEG)
                ref[base + j, :, piece] = jnp.where(
                    cuts[j] < length // 2, back[at : at + 2 * levs], ref[base + j, :, piece]
                )

    tiles = rows + rows // 2
    low_lane = lax.broadcasted_iota(jnp.int32, (2 * levs, 128), 1) < 64

    def encode(slot, parts):
        most = jnp.abs(parts[0])
        for part in parts[1:]:
            most = jnp.maximum(most, jnp.abs(part))
        most = jnp.maximum(jnp.max(most, axis=0, keepdims=True), 1e-30)
        to_code = CODE_MAX / most
        send_scale[slot] = most * (1.0 / CODE_MAX)
        for a, part in enumerate(parts):
            code = (part * to_code + ROUNDER) - ROUNDER
            send[slot, a] = code.astype(jnp.int32).astype(jnp.int16)

    def pack(e):
        def tile(j, t):
            return u[j, :, pl.ds(pl.multiple_of(e * width + t * 128, 128), 128)]

        first = [tile(j, 0) for j in range(rows)]
        second = [tile(j, 2) for j in range(rows)]
        for j in range(0, rows, 2):
            one, two = tile(j, 1), tile(j + 1, 1)
            first.append(jnp.where(low_lane, one, pltpu.roll(two, 64, 1)))
            second.append(jnp.where(low_lane, pltpu.roll(one, 64, 1), two))
        encode(2 * e, first)
        encode(2 * e + 1, second)

    def target(step):
        half = lax.div(step + 1, 2)
        return lax.rem(y + n_y // 2 + jnp.where(lax.rem(step, 2) == 1, -half, half), n_y)

    def column_copies(step, core):
        other = target(step) * 2 + core
        return [
            pltpu.make_async_remote_copy(
                src_ref=source.at[other], dst_ref=goal.at[ilev],
                send_sem=sent.at[step, core], recv_sem=got.at[step, parity],
                device_id={"lev": other}, device_id_type=MESH,
            )
            for source, goal, sent, got in (
                (send_scale, recv_scale, scale_sent, scale_got),
                (send, recv, a2a_send, a2a_recv),
            )
        ]

    def column_start(step, core):
        for copy in column_copies(step, core):
            copy.start()

    def column_wait(step, core):
        for source, goal, sent, got in (
            (send_scale, recv_scale, scale_sent, scale_got),
            (send, recv, a2a_send, a2a_recv),
        ):
            pltpu.make_async_remote_copy(
                src_ref=source.at[0], dst_ref=goal.at[ilev],
                send_sem=sent.at[step, core], recv_sem=got.at[step, core],
                device_id={"lev": ilev}, device_id_type=MESH,
            ).wait_recv()

    def decode(chip):
        for a in range(tiles):
            parts = []
            for core in range(2):
                code = recv[2 * chip + core, a].astype(jnp.int32).astype(F32)
                parts.append(code * recv_scale[2 * chip + core])
            high, low = halves(jnp.concatenate(parts, axis=0))
            at = pl.ds(pl.multiple_of(chip * 4 * levs, 4 * levs), 4 * levs)
            x_high[at, a * 128 : (a + 1) * 128] = high
            x_low[at, a * 128 : (a + 1) * 128] = low

    def columns(before):
        @pl.loop(0, n_y - 1)
        def _(step):
            e = target(step)
            before(e)
            pack(e)
            column_start(step, 0)
            column_start(step, 1)

        before(y)
        pack(y)
        column_start(n_y - 1, 1 - parity)
        recv[ilev] = send[ilev]
        recv_scale[ilev] = send_scale[ilev]

    loads[2].wait()
    halo_start(0, 1)
    for load in loads[3:]:
        load.start()
    for load in loads[:2]:
        load.wait()
    send_near(0)
    send_near(1)
    halo_start(1, 3)
    stage[0, 0] = u[rows - 2].astype(BF16)
    stage[1, 0] = u[1].astype(BF16)
    halo_start(3, 4)
    for r in range(rows):
        set_coef_x(r)
        z[r] = zonal(u[r], coef_x[r])
    for r in range(rows - 1):
        set_coef_y(r)
    pieces(own_part)
    halo_start(4, 5)
    tell(ring_one, lev=level(1, parity))
    tell(ring_one, lev=level(-1, parity))
    for load in loads[3:]:
        load.wait()
    write_maps(n_lev, levs, wv, maps)
    halo_wait(1)
    first_substep(1)
    pl.semaphore_wait(ring_one, 2)
    tell(ring_two, lev=level(2, parity))
    tell(ring_two, lev=level(-2, parity))
    halo_wait(0)
    first_substep(0)
    pl.semaphore_wait(ring_two, 2)
    is_polar = jnp.logical_or(ilat < polar, ilat >= n_lat - polar)

    @pl.when(is_polar)
    def _():
        pieces(second_part)
        low_pass(u, 0, 0)
        columns(lambda e: None)

    @pl.when(jnp.logical_not(is_polar))
    def _():
        columns(lambda e: second_part(pl.ds(pl.multiple_of(e * width, 128), width)))

    for side in (0, 1):

        @pl.when(there[side])
        def _():
            for copy in halo_copies(side):
                copy.wait_send()

    column_wait(n_y - 1, 1 - parity)
    decode(y)

    @pl.loop(1, n_y)
    def _(lap):
        step = n_y - 1 - lap
        column_wait(step, 0)
        column_wait(step, 1)
        decode(lax.rem(2 * y + n_y - target(step), n_y))

    @pl.loop(0, n_y - 1)
    def _(step):
        for core in range(2):
            for copy in column_copies(step, core):
                copy.wait_send()

    for copy in column_copies(n_y - 1, 1 - parity):
        copy.wait_send()


def write_maps(n_lev, levs, wv, maps):
    count = n_lev * levs
    depth = n_lev * 2 * levs
    source = lax.broadcasted_iota(jnp.int32, (count, depth), 1)
    goal = lax.broadcasted_iota(jnp.int32, (count, depth), 0)
    level = lax.div(source, 2 * levs) * levs + lax.rem(source, levs)
    is_heat = lax.rem(source, 2 * levs) >= levs
    scale = count**-0.5
    deeper = jnp.where(level > goal, scale, jnp.where(level == goal, 0.5 * scale, 0.0))
    w_high, w_low = halves(wv[...])
    one_hot = (level == goal).astype(F32).astype(BF16)
    for half, w in enumerate((w_high, w_low)):
        wide = jnp.dot(w, one_hot, preferred_element_type=F32)
        maps[half, 0:count, :] = jnp.where(is_heat, 0.0, wide).astype(BF16)
        maps[half, count : 2 * count, :] = jnp.where(is_heat, wide, 0.0).astype(BF16)
    maps[0, 2 * count : 3 * count, :] = jnp.where(is_heat, deeper, 0.0).astype(BF16)
    maps[1, 2 * count : 3 * count, :] = jnp.zeros((count, depth), BF16)


def remap(x_high, x_low, maps, surf, out, geo, out_v, geo_v, out_sem, geo_sem):
    rows = surf.shape[0]
    count = maps.shape[1] // 3
    parity = lax.rem(lax.axis_index("lev"), 2)
    y = jnp.dot(maps[0], x_high[...], preferred_element_type=F32)
    y += jnp.dot(maps[0], x_low[...], preferred_element_type=F32)
    y += jnp.dot(maps[1], x_high[...], preferred_element_type=F32)
    low_out = lax.broadcasted_iota(jnp.int32, (count, 128), 1) < 64

    def put(j, f, first, second):
        if f < 2:
            out_v[f, j, :, 0:128] = first
            out_v[f, j, :, 128:192] = second[:, 0:64]
            pltpu.make_async_copy(out_v.at[f, j], out.at[f, j], out_sem.at[f, j]).start()
        else:
            geo_v[j, :, 0:128] = first
            geo_v[j, :, 128:192] = second[:, 0:64]
            pltpu.make_async_copy(geo_v.at[j], geo.at[j], geo_sem.at[j]).start()

    @pl.when(parity == 0)
    def _():
        for j in range(rows):
            for f in range(3):
                main = y[f * count : (f + 1) * count, j * 128 : (j + 1) * 128]
                at = (rows + j // 2) * 128
                side = y[f * count : (f + 1) * count, at : at + 128]
                if j % 2 == 1:
                    side = pltpu.roll(side, 64, 1)
                if f == 2:
                    main = main + surf[j : j + 1, 0:128]
                    side = side + surf[j : j + 1, 128:256]
                put(j, f, main, side)

    @pl.when(parity == 1)
    def _():
        for j in range(rows):
            for f in range(3):
                main = y[f * count : (f + 1) * count, j * 128 : (j + 1) * 128]
                at = (rows + j // 2) * 128
                side = y[f * count : (f + 1) * count, at : at + 128]
                if f == 2:
                    main = main + surf[j : j + 1, 256:384]
                    ground = surf[j : j + 1, 128:256]
                    side = side + (pltpu.roll(ground, 64, 1) if j % 2 == 0 else ground)
                if j % 2 == 1:
                    side = pltpu.roll(side, 64, 1)
                main = pltpu.roll(main, 64, 1)
                put(j, f, jnp.where(low_out, side, main), main)

    for j in range(rows):
        for f in range(2):
            pltpu.make_async_copy(out_v.at[f, j], out.at[f, j], out_sem.at[f, j]).wait()
        pltpu.make_async_copy(geo_v.at[j], geo.at[j], geo_sem.at[j]).wait()


def solution(mesh):
    n_lat, n_lev = mesh.shape["lat"], mesh.shape["lev"]

    def shards(fields, courant, cutoffs, surface, weights):
        _, rows, levs, length = fields.shape
        fwd, inv, turn = fourier_tables(length)
        count = weights.shape[0]
        tiles = rows + rows // 2
        hbm_spec = pl.BlockSpec(memory_space=pltpu.HBM)
        vmem_spec = pl.BlockSpec(memory_space=pltpu.VMEM)
        dma = pltpu.SemaphoreType.DMA
        parts = pl.pallas_call(
            functools.partial(transport, n_lat, n_lev, 16 // rows),
            name="transport",
            out_shape=(
                pltpu.VMEM((2 * count, tiles * 128), BF16),
                pltpu.VMEM((2 * count, tiles * 128), BF16),
                pltpu.VMEM((2, 3 * count, 2 * count), BF16),
                pltpu.VMEM((rows, 384), F32),
            ),
            in_specs=[hbm_spec] * 8,
            out_specs=(vmem_spec,) * 4,
            scratch_shapes=[
                pltpu.VMEM(courant.shape, BF16),
                pltpu.SMEM(cutoffs.shape, jnp.int32),
                pltpu.VMEM(weights.shape, F32),
                pltpu.VMEM(fwd.shape, BF16),
                pltpu.VMEM(inv.shape, BF16),
                pltpu.VMEM(turn.shape, F32),
                pltpu.VMEM((rows, 2 * levs, length), F32),
                pltpu.VMEM((rows + 4, 2 * levs, length), F32),
                pltpu.VMEM((rows, 2 * levs, length), F32),
                pltpu.VMEM((rows, 2 * levs, length), F32),
                pltpu.VMEM((rows + 3, 2 * levs, length), F32),
                pltpu.VMEM((2, 2 * levs, length), F32),
                pltpu.VMEM((2, 2 * levs, length), jnp.int16),
                pltpu.VMEM((2, 2 * levs, length), jnp.int16),
                pltpu.VMEM((2, 2, 1, 128), F32),
                pltpu.VMEM((2, 3, 2 * levs, length), BF16),
                pltpu.VMEM((2, 3, 2 * levs, length), BF16),
                pltpu.VMEM((2, 2, levs, length), BF16),
                pltpu.VMEM((n_lev, tiles, 2 * levs, 128), jnp.int16),
                pltpu.VMEM((n_lev, tiles, 2 * levs, 128), jnp.int16),
                pltpu.VMEM((n_lev, 1, 128), F32),
                pltpu.VMEM((n_lev, 1, 128), F32),
                dma((9,)),
                dma((2, 5)),
                dma((2, 5)),
                dma((n_lev // 2, 2)),
                dma((n_lev // 2, 2)),
                dma((n_lev // 2, 2)),
                dma((n_lev // 2, 2)),
                pltpu.SemaphoreType.REGULAR,
                pltpu.SemaphoreType.REGULAR,
            ],
            compiler_params=pltpu.CompilerParams(
                collective_id=0, has_side_effects=True
            ),
        )(fields, courant, cutoffs, surface, weights, fwd, inv, turn)
        columns = length // n_lev
        return pl.pallas_call(
            remap,
            name="remap",
            out_shape=(
                jax.ShapeDtypeStruct((2, rows, count, columns), F32),
                jax.ShapeDtypeStruct((rows, count, columns), F32),
            ),
            in_specs=[vmem_spec] * 4,
            out_specs=(hbm_spec, hbm_spec),
            scratch_shapes=[
                pltpu.VMEM((2, rows, count, columns), F32),
                pltpu.VMEM((rows, count, columns), F32),
                dma((2, rows)),
                dma((rows,)),
            ],
            compiler_params=pltpu.CompilerParams(vmem_limit_bytes=24 << 20),
        )(*parts)

    return jax.shard_map(
        shards,
        mesh=mesh,
        in_specs=(
            P(None, "lat", "lev", None),
            P(None, "lat", "lev", None),
            P(),
            P("lat", None),
            P(),
        ),
        out_specs=(P(None, "lat", None, "lev"), P("lat", None, "lev")),
        check_vma=False,
    )
```

```python
import functools

import jax
import jax.numpy as jnp
import numpy as np
from jax import lax
from jax.experimental import pallas as pl
from jax.experimental.pallas import tpu as pltpu
from jax.sharding import PartitionSpec as P

MESH = pl.DeviceIdType.MESH
KMAX = 128
SEG = 256
CODE_MAX = 32767.0
ROUNDER = 1.5 * 2.0**23
F32 = jnp.float32
BF16 = jnp.bfloat16


def split_bf16(table):
    high = table.astype(np.float32).astype(jnp.bfloat16)
    low = (table - high.astype(np.float64)).astype(np.float32).astype(jnp.bfloat16)
    return np.stack([high, low])


def fourier_tables(length):
    waves = np.arange(KMAX)
    phase = (np.arange(SEG)[:, None] * waves[None, :]) % length
    angle = phase * (2.0 * np.pi / length)
    inner = np.concatenate([np.cos(angle), np.sin(angle)], axis=1)
    segments = length // SEG
    outer = (np.arange(segments)[:, None] * waves[None, :]) % segments
    outer = outer * (2.0 * np.pi / segments)
    turn = np.stack([np.cos(outer), np.sin(outer)], axis=1).astype(np.float32)
    return split_bf16(inner), split_bf16(inner.T), turn.reshape(2 * segments, KMAX)


def halves(x):
    high = x.astype(BF16)
    return high, (x - high.astype(F32)).astype(BF16)


def dot3(x, high, low):
    x_high, x_low = halves(x)
    out = jnp.dot(x_high, high, preferred_element_type=F32)
    out += jnp.dot(x_low, high, preferred_element_type=F32)
    return out + jnp.dot(x_high, low, preferred_element_type=F32)


def zonal(u, coef):
    length = u.shape[-1]
    pair = u + pltpu.roll(u, length - 1, 1)
    face = 8.0 * pair - (pltpu.roll(pair, 1, 1) + pltpu.roll(pair, length - 1, 1))
    flux = coef * face
    return u - (flux - pltpu.roll(flux, 1, 1))


def transport(
    n_lat, n_lev, polar,
    fields, courant, cutoffs, surface, weights, fwd, inv, turn,
    x_high, x_low, maps, surf,
    cv, cut, wv, fwd_v, inv_v, turn_v,
    u, v, z, coef_x, coef_y, near, near_sent, near_got, near_scale, far, stage, cy_halo, send, recv, send_scale, recv_scale,
    in_sem, halo_send, halo_recv, a2a_send, a2a_recv, scale_sent, scale_got,
    ring_one, ring_two,
):
    ilat, ilev = lax.axis_index("lat"), lax.axis_index("lev")
    rows, length = u.shape[0], u.shape[2]
    levs = u.shape[1] // 2
    segments = length // SEG
    n_y = n_lev // 2
    y, parity = lax.div(ilev, 2), lax.rem(ilev, 2)
    width = 3 * 128

    loads = [
        pltpu.make_async_copy(fields.at[0], u.at[:, 0:levs, :], in_sem.at[0]),
        pltpu.make_async_copy(fields.at[1], u.at[:, levs : 2 * levs, :], in_sem.at[1]),
        pltpu.make_async_copy(courant, cv, in_sem.at[2]),
        pltpu.make_async_copy(weights, wv, in_sem.at[5]),
        pltpu.make_async_copy(cutoffs, cut, in_sem.at[3]),
        pltpu.make_async_copy(
            surface.at[:, pl.ds(pl.multiple_of(y * width, 128), width)], surf, in_sem.at[4]
        ),
        pltpu.make_async_copy(fwd, fwd_v, in_sem.at[6]),
        pltpu.make_async_copy(inv, inv_v, in_sem.at[7]),
        pltpu.make_async_copy(turn, turn_v, in_sem.at[8]),
    ]

    for n in (2, 0, 1):
        loads[n].start()

    has_minus, has_plus = ilat > 0, ilat < n_lat - 1
    barrier = pltpu.get_barrier_semaphore()

    def tell(sem, **where):
        pl.semaphore_signal(sem, inc=1, device_id=where, device_id_type=MESH)

    def level(step, core):
        return lax.rem(y + step + n_y, n_y) * 2 + core

    @pl.when(has_minus)
    def _():
        tell(barrier, lat=ilat - 1)

    @pl.when(has_plus)
    def _():
        tell(barrier, lat=ilat + 1)

    for core in range(2):
        tell(barrier, lev=level(1, core))
        tell(barrier, lev=level(-1, core))
    tell(barrier, lev=level(0, 1 - parity))

    neighbours = has_minus.astype(jnp.int32) + has_plus.astype(jnp.int32)
    pl.semaphore_wait(barrier, 5 + neighbours)

    def halo_copies(side):
        pieces = [
            (cv.at[1, pl.ds((rows - 2, 0)[side], 2)], cy_halo.at[side]),
            (near_scale.at[0, side], near_scale.at[1, side]),
            (near_sent.at[side], near_got.at[side]),
            (stage.at[side, 0], far.at[side, 0]),
            (stage.at[side, pl.ds(1, 2)], far.at[side, pl.ds(1, 2)]),
        ]
        return [
            pltpu.make_async_remote_copy(
                src_ref=source, dst_ref=goal,
                send_sem=halo_send.at[side, n], recv_sem=halo_recv.at[side, n],
                device_id={"lat": ilat + (1, -1)[side]}, device_id_type=MESH,
            )
            for n, (source, goal) in enumerate(pieces)
        ]

    there = (has_plus, has_minus)

    def halo_start(first, last):
        for side in (0, 1):

            @pl.when(there[side])
            def _():
                for copy in halo_copies(side)[first:last]:
                    copy.start()

    def halo_wait(side, first, last):
        @pl.when(there[1 - side])
        def _():
            for copy in halo_copies(side)[first:last]:
                copy.wait_recv()

        if first == 0:

            @pl.when(jnp.logical_not(there[1 - side]))
            def _():
                near_got[side] = jnp.zeros(near_got.shape[1:], jnp.int16)
                near_scale[1, side] = jnp.zeros(near_scale.shape[2:], F32)
                far[side] = jnp.zeros(far.shape[1:], BF16)
                cy_halo[side] = jnp.zeros(cy_halo.shape[1:], BF16)

    def both(x):
        return jnp.concatenate([x, x], axis=0)

    def cy_row(r):
        if r < 0:
            return both(cy_halo[0, r + 2].astype(F32))
        if r >= rows:
            return both(cy_halo[1, r - rows].astype(F32))
        return both(cv[1, r].astype(F32))

    def spans():
        return [slice(t * 128, (t + 1) * 128) for t in range(length // 128)]

    def send_near(side):
        row = (rows - 1, 0)[side]
        most = jnp.full((2 * levs, 128), 1e-30, F32)
        for at in spans():
            most = jnp.maximum(most, jnp.abs(u[row, :, at]))
        most = jnp.max(most, axis=0, keepdims=True)
        near_scale[0, side] = most * (1.0 / CODE_MAX)
        to_code = CODE_MAX / most
        for at in spans():
            code = (u[row, :, at] * to_code + ROUNDER) - ROUNDER
            near_sent[side, :, at] = code.astype(jnp.int32).astype(jnp.int16)

    def take_near(side):
        for at in spans():
            near[side, :, at] = near_got[side, :, at].astype(jnp.int32).astype(F32) * near_scale[1, side]

    def v_row(r, at=slice(None)):
        return v[r + 2, :, at]

    def set_coef_x(r):
        cx = both(cv[0, r].astype(F32))
        coef_x[r] = (cx + pltpu.roll(cx, length - 1, 1)) * (1.0 / 24.0)

    def set_coef_y(r):
        coef_y[r + 2] = (cy_row(r) + cy_row(r + 1)) * (1.0 / 24.0)

    def pieces(body, piece=512):
        @pl.loop(0, length // piece)
        def _(c):
            body(pl.ds(pl.multiple_of(c * piece, 128), piece))

    def own_part(at):
        u0, u1, u2, u3 = (u[r, :, at] for r in range(4))
        low = coef_y[2, :, at] * (7.0 * (u0 + u1) - u2)
        middle = coef_y[3, :, at] * (7.0 * (u1 + u2) - (u0 + u3))
        high = coef_y[4, :, at] * (7.0 * (u2 + u3) - u1)
        z0, z1 = z[0, :, at] - low, z[1, :, at] - middle + low
        z2, z3 = z[2, :, at] - high + middle, z[3, :, at] + high
        z[0, :, at], z[1, :, at], z[2, :, at], z[3, :, at] = z0, z1, z2, z3
        stage[0, 1, :, at] = (z3 - u3).astype(BF16)
        stage[0, 2, :, at] = z2.astype(BF16)
        stage[1, 1, :, at] = (z0 - u0).astype(BF16)
        stage[1, 2, :, at] = z1.astype(BF16)

    places = (
        ((1, 0), (0, 1), (0, 1, 2), 1.0),
        ((rows + 2, rows + 3), (rows - 1, rows - 2), (rows + 2, rows + 1, rows), -1.0),
    )

    def inner_part(side, at):
        (outer, outermost), (edge, inner), (beyond, shared, inside), sign = places[side]
        n, f = near[side, :, at], far[side, 0, :, at].astype(F32)
        flux = coef_y[shared, :, at] * (7.0 * (n + u[edge, :, at]) - (f + u[inner, :, at]))
        mine = coef_y[inside, :, at] * n
        theirs = coef_y[beyond, :, at] * u[edge, :, at]
        v[edge + 2, :, at] = z[edge, :, at] + sign * (mine + flux)
        v[inner + 2, :, at] = z[inner, :, at] - sign * mine
        v[outer, :, at] = n - sign * (flux + theirs)
        v[outermost, :, at] = sign * theirs

    def outer_part(side, at):
        outer, outermost = places[side][0]
        v[outer, :, at] += far[side, 1, :, at].astype(F32)
        v[outermost, :, at] += far[side, 2, :, at].astype(F32)

    def second_part(first, at):
        full = [v_row(r, at) for r in range(first - 2, first + 4)]
        before = None
        for n in range(3):
            a, b, d, e = full[n : n + 4]
            r = first + n - 1
            flux = coef_y[r + 2, :, at] * (7.0 * (b + d) - (a + e))
            if before is not None:
                u[r, :, at] = z[r, :, at] - (flux - before)
            before = flux

    def band_is_polar(band):
        return jnp.logical_or(band < polar, band >= n_lat - polar)

    def second_zonal(first):
        for r in (first, first + 1):
            z[r] = zonal(v_row(r), coef_x[r])

    def first_inner(side):
        take_near(side)
        for r in ((-2, -1), (rows - 1, rows))[side]:
            set_coef_y(r)
        pieces(functools.partial(inner_part, side))

    def first_outer(side):
        pieces(functools.partial(outer_part, side))
        first = (-2, rows)[side]

        @pl.when(jnp.logical_not(there[1 - side]))
        def _():
            for r in (first, first + 1):
                v[r + 2] = jnp.zeros(v.shape[1:], F32)

        group = (-2, rows // 2)[side]
        other = ilat + (-1, 1)[side]

        @pl.when(jnp.logical_or(band_is_polar(ilat), band_is_polar(other)))
        def _():
            low_pass(v, group + 2, group)

    def low_pass(ref, base, first):
        x = jnp.concatenate([ref[base + j] for j in range(rows)], axis=0)
        cuts = [cut[jnp.clip(ilat * rows + first + j, 0, n_lat * rows - 1)] for j in range(rows)]
        count = x.shape[0]
        stacked = jnp.concatenate([x[:, q * SEG : (q + 1) * SEG] for q in range(segments)], axis=0)
        part = dot3(stacked, fwd_v[0], fwd_v[1])
        real = jnp.zeros((count, KMAX), F32)
        imag = jnp.zeros((count, KMAX), F32)
        for q in range(segments):
            p = part[q * count : (q + 1) * count, 0:KMAX]
            s = part[q * count : (q + 1) * count, KMAX : 2 * KMAX]
            c_q, s_q = turn_v[2 * q : 2 * q + 1, :], turn_v[2 * q + 1 : 2 * q + 2, :]
            real += c_q * p - s_q * s
            imag += s_q * p + c_q * s
        wave = lax.broadcasted_iota(jnp.int32, (2 * levs, KMAX), 1)
        double = jnp.where(wave == 0, 1.0 / length, 2.0 / length).astype(F32)
        weight = jnp.concatenate(
            [jnp.where(wave <= cuts[j], double, 0.0) for j in range(rows)], axis=0
        )
        real, imag = real * weight, imag * weight
        spread = []
        for q in range(segments):
            c_q, s_q = turn_v[2 * q : 2 * q + 1, :], turn_v[2 * q + 1 : 2 * q + 2, :]
            spread.append(
                jnp.concatenate([real * c_q + imag * s_q, imag * c_q - real * s_q], axis=1)
            )
        back = dot3(jnp.concatenate(spread, axis=0), inv_v[0], inv_v[1])
        for q in range(segments):
            for j in range(rows):
                at = q * count + j * 2 * levs
                piece = slice(q * SEG, (q + 1) * SEG)
                ref[base + j, :, piece] = jnp.where(
                    cuts[j] < length // 2, back[at : at + 2 * levs], ref[base + j, :, piece]
                )

    tiles = rows + rows // 2
    low_lane = lax.broadcasted_iota(jnp.int32, (2 * levs, 128), 1) < 64

    def encode(slot, half, parts):
        most = jnp.abs(parts[0])
        for part in parts[1:]:
            most = jnp.maximum(most, jnp.abs(part))
        most = jnp.maximum(jnp.max(most, axis=0, keepdims=True), 1e-30)
        to_code = CODE_MAX / most
        send_scale[slot, half] = most * (1.0 / CODE_MAX)
        for a, part in enumerate(parts):
            code = (part * to_code + ROUNDER) - ROUNDER
            send[slot, half, a] = code.astype(jnp.int32).astype(jnp.int16)

    def pack(e, half):
        def tile(j, t):
            return u[j, :, pl.ds(pl.multiple_of(e * width + t * 128, 128), 128)]

        j = 2 * half
        one, two = tile(j, 1), tile(j + 1, 1)
        lower = jnp.where(low_lane, one, pltpu.roll(two, 64, 1))
        upper = jnp.where(low_lane, pltpu.roll(one, 64, 1), two)
        encode(2 * e, half, [tile(j, 0), tile(j + 1, 0), lower])
        encode(2 * e + 1, half, [tile(j, 2), tile(j + 1, 2), upper])

    def target(step):
        half = lax.div(step + 1, 2)
        return lax.rem(y + n_y // 2 + jnp.where(lax.rem(step, 2) == 1, -half, half), n_y)

    def column_copies(half, step, core):
        other = target(step) * 2 + core
        return [
            pltpu.make_async_remote_copy(
                src_ref=source.at[other, half], dst_ref=goal.at[ilev, half],
                send_sem=sent.at[half, step, core], recv_sem=got.at[half, step, parity],
                device_id={"lev": other}, device_id_type=MESH,
            )
            for source, goal, sent, got in (
                (send_scale, recv_scale, scale_sent, scale_got),
                (send, recv, a2a_send, a2a_recv),
            )
        ]

    def column_start(half, step, core):
        for copy in column_copies(half, step, core):
            copy.start()

    def column_wait(half, step, core):
        for source, goal, sent, got in (
            (send_scale, recv_scale, scale_sent, scale_got),
            (send, recv, a2a_send, a2a_recv),
        ):
            pltpu.make_async_remote_copy(
                src_ref=source.at[0, half], dst_ref=goal.at[ilev, half],
                send_sem=sent.at[half, step, core], recv_sem=got.at[half, step, core],
                device_id={"lev": ilev}, device_id_type=MESH,
            ).wait_recv()

    def decode(half, chip):
        for n, a in enumerate((2 * half, 2 * half + 1, rows + half)):
            parts = []
            for core in range(2):
                code = recv[2 * chip + core, half, n].astype(jnp.int32).astype(F32)
                parts.append(code * recv_scale[2 * chip + core, half])
            high, low = halves(jnp.concatenate(parts, axis=0))
            at = pl.ds(pl.multiple_of(chip * 4 * levs, 4 * levs), 4 * levs)
            x_high[at, a * 128 : (a + 1) * 128] = high
            x_low[at, a * 128 : (a + 1) * 128] = low

    def columns(half, before):
        @pl.loop(0, n_y - 1)
        def _(step):
            e = target(step)
            before(e)
            pack(e, half)
            column_start(half, step, 0)
            column_start(half, step, 1)

        before(y)
        pack(y, half)
        column_start(half, n_y - 1, 1 - parity)
        recv[ilev, half] = send[ilev, half]
        recv_scale[ilev, half] = send_scale[ilev, half]

    def second_columns(half):
        columns(
            half,
            lambda e: second_part(2 * half, pl.ds(pl.multiple_of(e * width, 128), width)),
        )

    loads[2].wait()
    halo_start(0, 1)
    tell(ring_one, lev=level(1, parity))
    tell(ring_one, lev=level(-1, parity))
    for load in loads[3:]:
        load.start()
    for load in loads[:2]:
        load.wait()
    send_near(0)
    send_near(1)
    halo_start(1, 3)
    stage[0, 0] = u[rows - 2].astype(BF16)
    stage[1, 0] = u[1].astype(BF16)
    halo_start(3, 4)
    for r in range(rows):
        set_coef_x(r)
        z[r] = zonal(u[r], coef_x[r])
    for r in range(rows - 1):
        set_coef_y(r)
    pieces(own_part)
    halo_start(4, 5)
    for load in loads[3:]:
        load.wait()
    write_maps(n_lev, levs, wv, maps)
    pl.semaphore_wait(ring_one, 2)
    tell(ring_two, lev=level(2, parity))
    tell(ring_two, lev=level(-2, parity))
    is_polar = band_is_polar(ilat)
    halo_wait(1, 0, 5)
    first_inner(1)
    first_outer(1)
    second_zonal(2)
    halo_wait(0, 0, 4)
    first_inner(0)
    pl.semaphore_wait(ring_two, 2)

    @pl.when(jnp.logical_not(is_polar))
    def _():
        second_zonal(0)
        second_columns(1)

    halo_wait(0, 4, 5)
    first_outer(0)

    @pl.when(jnp.logical_not(is_polar))
    def _():
        second_columns(0)

    @pl.when(is_polar)
    def _():
        second_zonal(0)
        pieces(functools.partial(second_part, 2))
        pieces(functools.partial(second_part, 0))
        low_pass(u, 0, 0)
        columns(1, lambda e: None)
        columns(0, lambda e: None)

    for side in (0, 1):

        @pl.when(there[side])
        def _():
            for copy in halo_copies(side):
                copy.wait_send()

    for half in (1, 0):
        column_wait(half, n_y - 1, 1 - parity)
        decode(half, y)

        @pl.loop(1, n_y)
        def _(lap):
            step = n_y - 1 - lap
            column_wait(half, step, 0)
            column_wait(half, step, 1)
            decode(half, lax.rem(2 * y + n_y - target(step), n_y))

    for half in (1, 0):

        @pl.loop(0, n_y - 1)
        def _(step):
            for core in range(2):
                for copy in column_copies(half, step, core):
                    copy.wait_send()

        for copy in column_copies(half, n_y - 1, 1 - parity):
            copy.wait_send()


def write_maps(n_lev, levs, wv, maps):
    count = n_lev * levs
    depth = n_lev * 2 * levs
    source = lax.broadcasted_iota(jnp.int32, (count, depth), 1)
    goal = lax.broadcasted_iota(jnp.int32, (count, depth), 0)
    level = lax.div(source, 2 * levs) * levs + lax.rem(source, levs)
    is_heat = lax.rem(source, 2 * levs) >= levs
    scale = count**-0.5
    deeper = jnp.where(level > goal, scale, jnp.where(level == goal, 0.5 * scale, 0.0))
    w_high, w_low = halves(wv[...])
    one_hot = (level == goal).astype(F32).astype(BF16)
    for half, w in enumerate((w_high, w_low)):
        wide = jnp.dot(w, one_hot, preferred_element_type=F32)
        maps[half, 0:count, :] = jnp.where(is_heat, 0.0, wide).astype(BF16)
        maps[half, count : 2 * count, :] = jnp.where(is_heat, wide, 0.0).astype(BF16)
    maps[0, 2 * count : 3 * count, :] = jnp.where(is_heat, deeper, 0.0).astype(BF16)
    maps[1, 2 * count : 3 * count, :] = jnp.zeros((count, depth), BF16)


def remap(x_high, x_low, maps, surf, out, geo, out_v, geo_v, out_sem, geo_sem):
    rows = surf.shape[0]
    count = maps.shape[1] // 3
    parity = lax.rem(lax.axis_index("lev"), 2)
    y = jnp.dot(maps[0], x_high[...], preferred_element_type=F32)
    y += jnp.dot(maps[0], x_low[...], preferred_element_type=F32)
    y += jnp.dot(maps[1], x_high[...], preferred_element_type=F32)
    low_out = lax.broadcasted_iota(jnp.int32, (count, 128), 1) < 64

    def put(j, f, first, second):
        if f < 2:
            out_v[f, j, :, 0:128] = first
            out_v[f, j, :, 128:192] = second[:, 0:64]
            pltpu.make_async_copy(out_v.at[f, j], out.at[f, j], out_sem.at[f, j]).start()
        else:
            geo_v[j, :, 0:128] = first
            geo_v[j, :, 128:192] = second[:, 0:64]
            pltpu.make_async_copy(geo_v.at[j], geo.at[j], geo_sem.at[j]).start()

    @pl.when(parity == 0)
    def _():
        for j in range(rows):
            for f in range(3):
                main = y[f * count : (f + 1) * count, j * 128 : (j + 1) * 128]
                at = (rows + j // 2) * 128
                side = y[f * count : (f + 1) * count, at : at + 128]
                if j % 2 == 1:
                    side = pltpu.roll(side, 64, 1)
                if f == 2:
                    main = main + surf[j : j + 1, 0:128]
                    side = side + surf[j : j + 1, 128:256]
                put(j, f, main, side)

    @pl.when(parity == 1)
    def _():
        for j in range(rows):
            for f in range(3):
                main = y[f * count : (f + 1) * count, j * 128 : (j + 1) * 128]
                at = (rows + j // 2) * 128
                side = y[f * count : (f + 1) * count, at : at + 128]
                if f == 2:
                    main = main + surf[j : j + 1, 256:384]
                    ground = surf[j : j + 1, 128:256]
                    side = side + (pltpu.roll(ground, 64, 1) if j % 2 == 0 else ground)
                if j % 2 == 1:
                    side = pltpu.roll(side, 64, 1)
                main = pltpu.roll(main, 64, 1)
                put(j, f, jnp.where(low_out, side, main), main)

    for j in range(rows):
        for f in range(2):
            pltpu.make_async_copy(out_v.at[f, j], out.at[f, j], out_sem.at[f, j]).wait()
        pltpu.make_async_copy(geo_v.at[j], geo.at[j], geo_sem.at[j]).wait()


def solution(mesh):
    n_lat, n_lev = mesh.shape["lat"], mesh.shape["lev"]

    def shards(fields, courant, cutoffs, surface, weights):
        _, rows, levs, length = fields.shape
        fwd, inv, turn = fourier_tables(length)
        count = weights.shape[0]
        tiles = rows + rows // 2
        hbm_spec = pl.BlockSpec(memory_space=pltpu.HBM)
        vmem_spec = pl.BlockSpec(memory_space=pltpu.VMEM)
        dma = pltpu.SemaphoreType.DMA
        parts = pl.pallas_call(
            functools.partial(transport, n_lat, n_lev, 16 // rows),
            name="transport",
            out_shape=(
                pltpu.VMEM((2 * count, tiles * 128), BF16),
                pltpu.VMEM((2 * count, tiles * 128), BF16),
                pltpu.VMEM((2, 3 * count, 2 * count), BF16),
                pltpu.VMEM((rows, 384), F32),
            ),
            in_specs=[hbm_spec] * 8,
            out_specs=(vmem_spec,) * 4,
            scratch_shapes=[
                pltpu.VMEM(courant.shape, BF16),
                pltpu.SMEM(cutoffs.shape, jnp.int32),
                pltpu.VMEM(weights.shape, F32),
                pltpu.VMEM(fwd.shape, BF16),
                pltpu.VMEM(inv.shape, BF16),
                pltpu.VMEM(turn.shape, F32),
                pltpu.VMEM((rows, 2 * levs, length), F32),
                pltpu.VMEM((rows + 4, 2 * levs, length), F32),
                pltpu.VMEM((rows, 2 * levs, length), F32),
                pltpu.VMEM((rows, 2 * levs, length), F32),
                pltpu.VMEM((rows + 3, 2 * levs, length), F32),
                pltpu.VMEM((2, 2 * levs, length), F32),
                pltpu.VMEM((2, 2 * levs, length), jnp.int16),
                pltpu.VMEM((2, 2 * levs, length), jnp.int16),
                pltpu.VMEM((2, 2, 1, 128), F32),
                pltpu.VMEM((2, 3, 2 * levs, length), BF16),
                pltpu.VMEM((2, 3, 2 * levs, length), BF16),
                pltpu.VMEM((2, 2, levs, length), BF16),
                pltpu.VMEM((n_lev, 2, tiles // 2, 2 * levs, 128), jnp.int16),
                pltpu.VMEM((n_lev, 2, tiles // 2, 2 * levs, 128), jnp.int16),
                pltpu.VMEM((n_lev, 2, 1, 128), F32),
                pltpu.VMEM((n_lev, 2, 1, 128), F32),
                dma((9,)),
                dma((2, 5)),
                dma((2, 5)),
                dma((2, n_lev // 2, 2)),
                dma((2, n_lev // 2, 2)),
                dma((2, n_lev // 2, 2)),
                dma((2, n_lev // 2, 2)),
                pltpu.SemaphoreType.REGULAR,
                pltpu.SemaphoreType.REGULAR,
            ],
            compiler_params=pltpu.CompilerParams(
                collective_id=0, has_side_effects=True
            ),
        )(fields, courant, cutoffs, surface, weights, fwd, inv, turn)
        columns = length // n_lev
        return pl.pallas_call(
            remap,
            name="remap",
            out_shape=(
                jax.ShapeDtypeStruct((2, rows, count, columns), F32),
                jax.ShapeDtypeStruct((rows, count, columns), F32),
            ),
            in_specs=[vmem_spec] * 4,
            out_specs=(hbm_spec, hbm_spec),
            scratch_shapes=[
                pltpu.VMEM((2, rows, count, columns), F32),
                pltpu.VMEM((rows, count, columns), F32),
                dma((2, rows)),
                dma((rows,)),
            ],
            compiler_params=pltpu.CompilerParams(vmem_limit_bytes=24 << 20),
        )(*parts)

    return jax.shard_map(
        shards,
        mesh=mesh,
        in_specs=(
            P(None, "lat", "lev", None),
            P(None, "lat", "lev", None),
            P(),
            P("lat", None),
            P(),
        ),
        out_specs=(P(None, "lat", None, "lev"), P("lat", None, "lev")),
        check_vma=False,
    )
```
